512 devices in a mesh: wide: 64 (over y, z), narrow: 8 (over x, core).
Axes of the slice: x: 4, y: 8, z: 8, core: 2. Of those that a mesh axis runs over, the one named last changes fastest.
Arguments:
- haze_bin_mass: float32 [4096, 256, 128], P('wide', 'narrow'), may hold values from 0.05 to 2
- wind_speed: float32 [4096, 256], P('wide', 'narrow'), may hold values from 0.1 to 0.9
- vapour: float32 [4096, 256], P('wide', 'narrow'), may hold values from 0.2 to 2
- uptake_rates: float32 [128], replicated, may hold values from 0.05 to 1
- coag_left: float32 [128, 8], replicated, may hold values from -0.5 to 0.5
- coag_right: float32 [128, 8], replicated, may hold values from -0.5 to 0.5
- coag_gain: float32 [8, 128], replicated, may hold values from -2 to 2
- coag_loss: float32 [8, 128], replicated, may hold values from -2 to 2
- targets: int32 [4096, 1], replicated, may hold values from 0 to 63; in each aligned block of 64 rows (0 to 63, 64 to 127, ...) at most 2 rows name the same one
- upwind_blocks: int32 [4096], replicated, may hold values from 0 to 4095, as said below
Outputs:
- haze_output_slots: float32 [8192, 256, 128], P('wide', 'narrow')
- vapour_out: float32 [4096, 256], P('wide', 'narrow')
The draws below stay inside these ranges and needn't reach their ends.
Inputs may be any that keep to these rules, and one draw needn't show every extreme that they name: `targets`: among the 64 rows of one aligned block of rows no owner appears more than 2 times, and some owner appears exactly 2 times. upwind_blocks[b] // 64 equals b // 64, or the index one above or one below it, counted cyclically over the 64 owners.
All inputs are finite; a program needn't handle non-finite values.
Results may differ from the reference program's by a relative error of at most 0.000073.
Values sent between devices are 32-bit elements; how exact they have to be, the bound alone decides.
No kernel may reach another device: no remote copies, remote signals or barrier semaphores. Data moves between devices by JAX's collectives and lax.ppermute only.
A program may use at most 64 MiB of HBM per device.

```python
import math
import jax
import jax.numpy as jnp
import numpy as np
from jax import lax

BINS = 128
RANK = 8
BLK_DEV = 64
MOST = 2
SLOTS_PER_OWNER = 128
BLOCKS = 4096
CELLS = 256
N_WIDE = 64


def draw_upwind_blocks(key, part):
    owner_count = BLOCKS // BLK_DEV
    first_key = jax.random.fold_in(key, 11)
    second_key = jax.random.fold_in(key, 23)
    blocks_all = jnp.arange(BLOCKS, dtype=jnp.int32)
    owner_of = blocks_all // BLK_DEV
    offset = jax.random.randint(first_key, (BLOCKS,), -1, 2).astype(jnp.int32)
    within = jax.random.randint(second_key, (BLOCKS,), 0, BLK_DEV).astype(jnp.int32)
    offset = offset.at[0].set(-1).at[BLOCKS - 1].set(1)
    within = within.at[0].set(BLK_DEV - 1).at[BLOCKS - 1].set(0)
    upwind_owner_index = (owner_of + offset + owner_count) % owner_count
    return (upwind_owner_index * BLK_DEV + within).astype(jnp.int32)


def block_levels(stream_key, shape, cuts, least, top_value):
    def one(dim, blocks):
        steps = jax.random.uniform(jax.random.fold_in(jax.random.fold_in(stream_key, 6), dim), (blocks,), jnp.float32, least / len(cuts), top_value / len(cuts))
        return jnp.repeat(jnp.exp(steps), shape[dim] // blocks).reshape((-1,) + (1,) * (len(shape) - dim - 1))

    level = one(*cuts[0])
    for cut in cuts[1:]:
        level = level * one(*cut)
    return level


def routed_block(rng, own, number, rows, amount, top, bound, lean):
    sequence = jax.random.permutation(rng, amount)
    crowded, ordinary = load_shares(amount, rows * top, bound, lean, True), load_shares(amount, rows * top, bound, lean, False)
    places = jnp.arange(amount)

    def named(tallies, rotation):
        used = int((tallies > 0).sum())
        fixed = max(1, used // 4)
        shifted = fixed + (places - fixed + rotation * (used - fixed)) % max(1, amount - fixed)
        return jnp.zeros((amount,), jnp.int32).at[sequence[jnp.where(places < fixed, places, shifted)]].set(jnp.asarray(tallies, jnp.int32))

    tallies = jnp.where(number % 4 == 0, named(crowded, number // 4), named(ordinary, number - number // 4 - 1))
    mixed = jax.random.permutation(jax.random.fold_in(own, 3), amount)
    giver, sink = mixed[0:amount // 2 * 2:2], mixed[1:amount // 2 * 2:2]
    room = jnp.minimum(tallies[giver] - 1, bound - tallies[sink]) // 2
    room = jnp.where((giver == sequence[0]) | (sink == sequence[0]) | (tallies[sink] == 0), 0, jnp.maximum(room, 0))
    shifted = jax.random.randint(jax.random.fold_in(own, 4), (amount // 2,), 0, 1 << 20) % (room + 1)
    tallies = tallies.at[giver].add(-shifted).at[sink].add(shifted)
    labels = jnp.searchsorted(jnp.cumsum(tallies), jnp.arange(rows * top), side="right").astype(jnp.int32)
    table = labels.reshape(top, rows).T
    table = table[jax.random.permutation(jax.random.fold_in(own, 1), rows)]
    rotation = jax.random.randint(jax.random.fold_in(own, 2), (rows, 1), 0, top)
    return jnp.take_along_axis(table, (jnp.arange(top)[None, :] + rotation) % top, axis=1)


def load_shares(amount, total, bound, slope, full):
    loads = [(1 << 20) // math.isqrt(standing ** slope) + 1 for standing in range(1, amount + 1)]
    largest = bound if full else min(bound, max(-(-total // amount), total * loads[0] // sum(loads)))
    least = 1 if total - largest >= amount - 1 else 0
    counts, rest = [largest] + [least] * (amount - 1), total - largest - least * (amount - 1)
    while rest > 0:
        movable = [i for i in range(1, amount) if counts[i] < largest] or [i for i in range(1, amount) if counts[i] < bound]
        pool, remaining = sum([loads[i] for i in movable]), rest
        for i in movable:
            more = min(bound - counts[i], max(1, remaining * loads[i] // pool), rest)
            counts[i] = counts[i] + more
            rest = rest - more
    return np.array(counts)


def gaussian(own_key, shape, width, bound, kind=jnp.bfloat16):
    return jnp.clip(width * jax.random.normal(own_key, shape, jnp.float32), -bound, bound).astype(kind)


def setup_inputs(seed: int = 0) -> dict:
    splits = jax.random.split(jax.random.key(seed), 11)
    haze_bin_mass = jnp.clip(jnp.exp(math.log(2.0) - 3.6888794 * jax.random.uniform(splits[0], (BLOCKS, CELLS, BINS), jnp.float32) ** block_levels(splits[0], (BLOCKS, CELLS, BINS), ((0, 64), (1, 8)), -0.2, 0.2)), 0.05, 2.0)
    wind_speed = jnp.clip(0.1 + 0.79999997 * jax.random.uniform(splits[1], (BLOCKS, CELLS), jnp.float32) ** block_levels(splits[1], (BLOCKS, CELLS), ((0, 64), (1, 8)), -0.2, 0.2), 0.1, 0.9)
    vapour = jnp.clip(jnp.exp(math.log(2.0) - 2.3025851 * jax.random.uniform(splits[2], (BLOCKS, CELLS), jnp.float32) ** block_levels(splits[2], (BLOCKS, CELLS), ((0, 64), (1, 8)), -0.2, 0.2)), 0.2, 2.0)
    uptake_rates = jnp.clip(jnp.exp(jax.random.uniform(splits[3], (BINS,), jnp.float32, math.log(0.05), math.log(1.0))), 0.05, 1.0)
    coag_left = gaussian(splits[4], (BINS, RANK), BINS ** -0.5, 0.5, jnp.float32)
    coag_right = gaussian(splits[5], (BINS, RANK), BINS ** -0.5, 0.5, jnp.float32)
    coag_gain = gaussian(splits[6], (RANK, BINS), RANK ** -0.5, 2.0, jnp.float32)
    coag_loss = gaussian(splits[7], (RANK, BINS), RANK ** -0.5, 2.0, jnp.float32)
    targets_keys = jax.random.split(jax.random.fold_in(splits[8], 1), BLOCKS // BLK_DEV)
    targets_turns = jax.random.permutation(jax.random.fold_in(splits[8], 3), BLOCKS // BLK_DEV)
    targets = jax.vmap(lambda own, number: routed_block(jax.random.fold_in(splits[8], 2), own, number, BLK_DEV, N_WIDE, 1, MOST, 2))(targets_keys, targets_turns).reshape((BLOCKS, 1))
    upwind_blocks = draw_upwind_blocks(jax.random.fold_in(splits[10], 71), 0)
    return {"haze_bin_mass": haze_bin_mass, "wind_speed": wind_speed, "vapour": vapour, "uptake_rates": uptake_rates, "coag_left": coag_left, "coag_right": coag_right, "coag_gain": coag_gain, "coag_loss": coag_loss, "targets": targets, "upwind_blocks": upwind_blocks}


PRECISE = lax.Precision.HIGHEST
STEP_DT = 0.25


def microphysics(haze_bin_mass, vapour, uptake_rates, coag_left, coag_right, coag_gain, coag_loss):
    flat_rows = haze_bin_mass.reshape(-1, haze_bin_mass.shape[-1])
    left_proj = jnp.dot(flat_rows, coag_left, precision=PRECISE, preferred_element_type=jnp.float32)
    right_proj = jnp.dot(flat_rows, coag_right, precision=PRECISE, preferred_element_type=jnp.float32)
    coagulation_kernel_rate = jnp.dot(left_proj * right_proj, coag_gain, precision=PRECISE, preferred_element_type=jnp.float32)
    coagulation_kernel_rate = coagulation_kernel_rate - flat_rows * jnp.dot(left_proj, coag_loss, precision=PRECISE, preferred_element_type=jnp.float32)
    coagulation_kernel_rate = coagulation_kernel_rate.reshape(haze_bin_mass.shape)
    mean_take = jnp.mean(haze_bin_mass * uptake_rates, axis=-1)
    factor = 1.0 / (1.0 + vapour * mean_take)
    uptake = (vapour * factor)[..., None] * uptake_rates * haze_bin_mass
    grown_mass = haze_bin_mass + STEP_DT * coagulation_kernel_rate + uptake
    return grown_mass, vapour * factor


def advect(grown_mass, inflow, wind_speed):
    upwind_row = jnp.concatenate([inflow[:, None, :], grown_mass[:, :-1, :]], axis=1)
    return grown_mass - wind_speed[..., None] * (grown_mass - upwind_row)


def slot_tables(targets, wide_count, block_dev):
    owner_table = targets[:, 0]
    capacity = max(2, 2 * block_dev // wide_count)
    grouped = owner_table.reshape(wide_count, block_dev)
    same_target = grouped[:, :, None] == grouped[:, None, :]
    positions = jnp.arange(block_dev)
    earlier = positions[None, :] < positions[:, None]
    rank_within = jnp.sum(same_target & earlier[None], axis=2).astype(jnp.int32).reshape(-1)
    source = (jnp.arange(owner_table.shape[0]) // block_dev).astype(jnp.int32)
    return owner_table, source * capacity + rank_within, capacity


def reference(haze_bin_mass, wind_speed, vapour, uptake_rates, coag_left, coag_right, coag_gain, coag_loss, targets, upwind_blocks):
    grown_mass, vapour_out = microphysics(haze_bin_mass, vapour, uptake_rates, coag_left, coag_right, coag_gain, coag_loss)
    inflow = grown_mass[upwind_blocks, grown_mass.shape[1] - 1, :]
    moved_mass = advect(grown_mass, inflow, wind_speed)
    owner_table, local_slot_index, capacity = slot_tables(targets, N_WIDE, BLK_DEV)
    global_slot_index = (owner_table * SLOTS_PER_OWNER + local_slot_index).astype(jnp.int32)
    haze_output_slots = jnp.zeros((N_WIDE * SLOTS_PER_OWNER, haze_bin_mass.shape[1], haze_bin_mass.shape[2]), jnp.float32)
    haze_output_slots = haze_output_slots.at[global_slot_index].set(moved_mass)
    return haze_output_slots, vapour_out
```

```python
import jax
import jax.numpy as jnp
from jax import lax
from jax.experimental import pallas as pl
from jax.experimental.pallas import tpu as pltpu
from jax.sharding import PartitionSpec as P

HIGHEST = lax.Precision.HIGHEST
STEP_DT = 0.25
F32 = jnp.float32
I32 = jnp.int32
VMEM = pltpu.VMEM


def precise_dot(a, b):
    return jnp.dot(a, b, precision=HIGHEST, preferred_element_type=F32)


def column_rows(table, column, rows, lanes):
    return jnp.broadcast_to(table[:, column : column + 1], (rows, lanes))


def fill_weights(first_rows, first_weights, second_weights, left, right, uptake, gain, loss):
    rank, bins = left.shape
    first_rows[...] = jnp.zeros_like(first_rows)
    first_rows[0:rank, :] = left
    first_rows[rank : 2 * rank, :] = left
    first_rows[bins : bins + rank, :] = right
    first_rows[2 * bins :, :] = jnp.broadcast_to(uptake * (1.0 / bins), (bins, bins))
    for k in range(3):
        first_weights[:, k * bins : (k + 1) * bins] = first_rows[k * bins : (k + 1) * bins, :].T
    second_weights[...] = jnp.zeros_like(second_weights)
    second_weights[0:rank, 0:bins] = STEP_DT * gain
    second_weights[rank : 2 * rank, bins:] = STEP_DT * loss


def weight_scratch(bins):
    return [
        pltpu.VMEM((3 * bins, bins), F32),
        pltpu.VMEM((bins, 3 * bins), F32),
        pltpu.VMEM((bins, 2 * bins), F32),
    ]


def rows_of_lanes(row, lanes):
    count = row.shape[1]
    shape = (count, count)
    eye = lax.broadcasted_iota(I32, shape, 0) == lax.broadcasted_iota(I32, shape, 1)
    spread = jnp.where(eye, jnp.broadcast_to(row, shape), 0.0)
    return precise_dot(spread, jnp.ones((count, lanes), F32))


def grow(x, vapour_rows, first_weights, second_weights, uptake, rank):
    rows, bins = x.shape
    lane = lax.broadcasted_iota(I32, (rows, bins), 1)
    one_lanes = jnp.where((lane >= rank) & (lane < 2 * rank), 1.0, 0.0).astype(F32)
    proj = precise_dot(x, first_weights[...])
    product = proj[:, :bins] * (proj[:, bins : 2 * bins] + one_lanes)
    rate = precise_dot(product, second_weights[...])
    taken = vapour_rows * (1.0 / (1.0 + vapour_rows * proj[:, 2 * bins :]))
    grown = x + (rate[:, :bins] - x * rate[:, bins:]) + taken * uptake * x
    return grown, taken


def rim_kernel(
    haze_hbm,
    vapour_ref,
    uptake_ref,
    left_ref,
    right_ref,
    gain_ref,
    loss_ref,
    rim_ref,
    rows_buf,
    first_rows,
    first_weights,
    second_weights,
    sem,
):
    cells = haze_hbm.shape[1]
    copy = pltpu.make_async_copy(haze_hbm.at[:, cells - 1, :], rows_buf, sem)
    copy.start()
    uptake = uptake_ref[...]
    weights = (left_ref[...], right_ref[...], uptake, gain_ref[...], loss_ref[...])
    fill_weights(first_rows, first_weights, second_weights, *weights)
    vapour_rows = rows_of_lanes(vapour_ref[cells - 1 : cells, :], rows_buf.shape[1])
    copy.wait()
    rim_ref[...], _ = grow(
        rows_buf[...], vapour_rows, first_weights, second_weights, uptake, left_ref.shape[0]
    )


def pack_kernel(
    haze_hbm,
    wind_ref,
    vapour_ref,
    uptake_ref,
    left_ref,
    right_ref,
    gain_ref,
    loss_ref,
    targets_hbm,
    upwind_hbm,
    packed_ref,
    top_ref,
    wind_top_ref,
    slot_ref,
    source_ref,
    haze_buf,
    first_rows,
    first_weights,
    second_weights,
    window,
    upwind_window,
    used,
    haze_sems,
    window_sems,
):
    blocks, cells, bins = haze_buf.shape
    rank = left_ref.shape[0]
    group = 8
    rows = group * cells
    wide_count = lax.axis_size("wide")
    owner = lax.axis_index("wide")
    first = lax.axis_index("narrow") == 0
    start = owner * blocks
    base = pl.multiple_of((start // 128) * 128, 128)
    far_base = pl.multiple_of((start // 1024) * 1024, 1024)
    window_copies = [
        pltpu.make_async_copy(targets_hbm.at[:, pl.ds(base, 128)], window, window_sems.at[0]),
        pltpu.make_async_copy(
            upwind_hbm.at[pl.ds(far_base, 1024)], upwind_window, window_sems.at[1]
        ),
    ]
    for copy in window_copies:
        copy.start()
    copies = []
    for g in range(blocks // group):
        part = pl.ds(g * group, group)
        copy = pltpu.make_async_copy(haze_hbm.at[part], haze_buf.at[part], haze_sems.at[g])
        copy.start()
        copies.append(copy)
    packed_ref[...] = jnp.zeros_like(packed_ref)
    for t in range(used.shape[0]):
        used[t] = 0
    uptake = uptake_ref[...]
    weights = (left_ref[...], right_ref[...], uptake, gain_ref[...], loss_ref[...])
    fill_weights(first_rows, first_weights, second_weights, *weights)
    top_row = lax.broadcasted_iota(I32, (rows, bins), 0) % cells == 0
    wind = wind_ref[...]
    vapour = vapour_ref[...]
    wind_top_ref[...] = rows_of_lanes(wind_ref[0:1, :], bins)
    for copy in window_copies:
        copy.wait()
    for g in range(blocks // group):
        copies[g].wait()
        x = haze_buf[g * group : (g + 1) * group].reshape(rows, bins)
        ids = range(g * group, (g + 1) * group)
        vapour_rows = jnp.concatenate([column_rows(vapour, b, cells, bins) for b in ids], 0)
        wind_rows = jnp.concatenate([column_rows(wind, b, cells, bins) for b in ids], 0)
        grown, _ = grow(x, vapour_rows, first_weights, second_weights, uptake, rank)
        upwind = jnp.where(top_row, 0.0, pltpu.roll(grown, 1, 0))
        moved = grown - wind_rows * (grown - upwind)
        for j, b in enumerate(ids):
            at = j * cells
            target = window[0, start - base + b]
            rank_within = used[target]
            used[target] = rank_within + 1
            slot = target * 2 + rank_within
            slot_ref[b] = slot
            packed_ref[slot] = moved[at : at + cells, :]
            top_ref[b : b + 1, :] = moved[at : at + 1, :]
            source = upwind_window[start - far_base + b]
            relative = lax.rem(source // blocks - owner + 1 + wide_count, wide_count)
            far = relative * blocks + lax.rem(source, blocks)
            source_ref[b] = jnp.where(first, far, blocks + b)


def inflow_kernel(
    packed_in,
    top_ref,
    wind_top_ref,
    same_ref,
    low_ref,
    high_ref,
    slot_ref,
    source_ref,
    packed_hbm,
    near,
    inflow,
    sem,
):
    blocks, bins = same_ref.shape
    near[0:blocks, :] = low_ref[...]
    near[blocks : 2 * blocks, :] = same_ref[...]
    near[2 * blocks :, :] = high_ref[...]
    for b in range(blocks):
        inflow[b : b + 1, :] = near[pl.ds(source_ref[b], 1), :]
    inflow[...] = top_ref[...] + wind_top_ref[...] * inflow[...]
    for b in range(blocks):
        pltpu.make_async_copy(inflow.at[b], packed_hbm.at[slot_ref[b], 0], sem).start()
    pltpu.make_async_copy(inflow, packed_hbm.at[pl.ds(0, blocks), 0, :], sem).wait()


def vapour_kernel(haze_ref, vapour_ref, uptake_ref, vapour_out_ref):
    blocks, cells, bins = haze_ref.shape
    vapour = vapour_ref[...]
    weights = jnp.broadcast_to(uptake_ref[...] * (1.0 / bins), (bins, bins)).T
    lane = lax.broadcasted_iota(I32, (cells, blocks), 1)
    out = jnp.zeros((cells, blocks), F32)
    for g in range(0, blocks, 8):
        mean_take = precise_dot(haze_ref[g : g + 8].reshape(8 * cells, bins), weights)
        for j in range(8):
            part = mean_take[j * cells : (j + 1) * cells, :blocks]
            out = jnp.where(lane == g + j, part, out)
    vapour_out_ref[...] = vapour * (1.0 / (1.0 + vapour * out))


def whole(space=VMEM):
    return pl.BlockSpec(memory_space=space)


def cost(flops, moved):
    return pl.CostEstimate(flops=flops, bytes_accessed=moved, transcendentals=0)


def local(
    haze_bin_mass,
    wind_speed,
    vapour,
    uptake_rates,
    coag_left,
    coag_right,
    coag_gain,
    coag_loss,
    targets,
    upwind_blocks,
):
    wide_count = lax.axis_size("wide")
    narrow_count = lax.axis_size("narrow")
    blocks, cells, bins = haze_bin_mass.shape
    slots = 2 * wide_count
    vapour_t = vapour.T
    uptake_row = uptake_rates[None, :]
    rates = (uptake_row, coag_left.T, coag_right.T, coag_gain, coag_loss)
    rim_type = jax.ShapeDtypeStruct((blocks, bins), F32)
    packed_type = jax.ShapeDtypeStruct((slots, cells, bins), F32)
    ids_type = jax.ShapeDtypeStruct((blocks,), I32)
    rim = pl.pallas_call(
        rim_kernel,
        out_shape=rim_type,
        in_specs=[whole(pl.ANY)] + [whole()] * 6,
        out_specs=whole(),
        scratch_shapes=[
            pltpu.VMEM((blocks, bins), F32),
            *weight_scratch(bins),
            pltpu.SemaphoreType.DMA,
        ],
        cost_estimate=cost(10000000, 100000),
    )(haze_bin_mass, vapour_t, *rates)
    last = narrow_count - 1
    both = ("wide", "narrow")
    along = [
        (w * narrow_count + n, w * narrow_count + (n + 1) % narrow_count)
        for w in range(wide_count)
        for n in range(narrow_count)
    ]
    up = [
        (w * narrow_count + last, ((w + 1) % wide_count) * narrow_count)
        for w in range(wide_count)
    ]
    down = [
        (w * narrow_count + last, ((w - 1) % wide_count) * narrow_count)
        for w in range(wide_count)
    ]
    low = lax.ppermute(rim, both, up)
    high = lax.ppermute(rim, both, down)
    same = lax.ppermute(rim, both, along)
    packed, top, wind_top, slot, source = pl.pallas_call(
        pack_kernel,
        out_shape=(packed_type, rim_type, rim_type, ids_type, ids_type),
        in_specs=[whole(pl.ANY)] + [whole()] * 7 + [whole(pl.ANY)] * 2,
        out_specs=(whole(),) * 3 + (whole(pltpu.SMEM),) * 2,
        scratch_shapes=[
            pltpu.VMEM((blocks, cells, bins), F32),
            *weight_scratch(bins),
            pltpu.SMEM((1, 128), I32),
            pltpu.SMEM((1024,), I32),
            pltpu.SMEM((wide_count,), I32),
            pltpu.SemaphoreType.DMA((blocks // 8,)),
            pltpu.SemaphoreType.DMA((2,)),
        ],
        cost_estimate=cost(800000000, 4000000),
        compiler_params=pltpu.CompilerParams(vmem_limit_bytes=67043328),
    )(haze_bin_mass, wind_speed.T, vapour_t, *rates, targets.T, upwind_blocks)
    packed = pl.pallas_call(
        inflow_kernel,
        out_shape=packed_type,
        in_specs=[whole(pl.ANY)] + [whole()] * 5 + [whole(pltpu.SMEM)] * 2,
        out_specs=whole(pl.ANY),
        scratch_shapes=[
            pltpu.VMEM((3 * blocks, bins), F32),
            pltpu.VMEM((blocks, bins), F32),
            pltpu.SemaphoreType.DMA,
        ],
        input_output_aliases={0: 0},
        cost_estimate=cost(100000, 300000),
    )(packed, top, wind_top, same, low, high, slot, source)
    haze_output_slots = lax.all_to_all(packed, "wide", split_axis=0, concat_axis=0, tiled=True)
    vapour_out = pl.pallas_call(
        vapour_kernel,
        out_shape=jax.ShapeDtypeStruct((cells, blocks), F32),
        in_specs=[whole()] * 3,
        out_specs=whole(),
        cost_estimate=cost(400000000, 1000000),
        compiler_params=pltpu.CompilerParams(vmem_limit_bytes=67043328),
    )(haze_bin_mass, vapour_t, uptake_row)
    return (haze_output_slots, vapour_out.T)


def solution(mesh):
    in_specs = (
        P("wide", "narrow", None),
        P("wide", "narrow"),
        P("wide", "narrow"),
        P(),
        P(),
        P(),
        P(),
        P(),
        P(),
        P(),
    )
    out_specs = (P("wide", "narrow", None), P("wide", "narrow"))
    return jax.shard_map(local, mesh=mesh, in_specs=in_specs, out_specs=out_specs, check_vma=False)
```

```python
import jax
import jax.numpy as jnp
from jax import lax
from jax.experimental import pallas as pl
from jax.experimental.pallas import tpu as pltpu
from jax.sharding import PartitionSpec as P

HIGHEST = lax.Precision.HIGHEST
STEP_DT = 0.25
F32 = jnp.float32
BF16 = jnp.bfloat16
I32 = jnp.int32
VMEM = pltpu.VMEM
SEGMENT = 32
TAKE_LANE = 24
COLUMNS = 8


def precise_dot(a, b):
    return jnp.dot(a, b, precision=HIGHEST, preferred_element_type=F32)


def split(x):
    high = x.astype(BF16)
    return high, (x - high.astype(F32)).astype(BF16)


def column_rows(table, column, rows, lanes):
    return jnp.broadcast_to(table[:, column : column + 1], (rows, lanes))


def rows_of_lanes(row, lanes):
    count = row.shape[1]
    shape = (count, count)
    eye = lax.broadcasted_iota(I32, shape, 0) == lax.broadcasted_iota(I32, shape, 1)
    spread = jnp.where(eye, jnp.broadcast_to(row, shape), 0.0)
    return precise_dot(spread, jnp.ones((count, lanes), F32))


def fill_weights(columns, second, first_both, first_low, second_ref, left, right, uptake, gain, loss):
    rank, bins = left.shape
    columns[...] = jnp.zeros_like(columns)
    for at in range(0, 3 * SEGMENT, SEGMENT):
        columns[at : at + rank, :] = left
        columns[at + rank : at + 2 * rank, :] = left
        columns[at + TAKE_LANE : at + TAKE_LANE + 1, :] = uptake * (1.0 / bins)
        columns[bins + at : bins + at + rank, :] = right
    for k in range(0, 2 * bins, bins):
        high, low = split(columns[k : k + bins, :].T)
        first_both[0:bins, k : k + bins] = high
        first_both[bins:, k : k + bins] = high
        first_low[:, k : k + bins] = low
    second[...] = jnp.zeros_like(second)
    second[0:rank, 0:bins] = STEP_DT * gain
    second[rank : 2 * rank, bins:] = STEP_DT * loss
    second[TAKE_LANE : TAKE_LANE + 1, bins:] = -uptake
    high, low = split(second[...])
    second_ref[0:SEGMENT, :] = high
    second_ref[SEGMENT : 2 * SEGMENT, :] = low
    second_ref[2 * SEGMENT : 3 * SEGMENT, :] = high
    second_ref[3 * SEGMENT :, :] = jnp.zeros_like(high)


def grow(x, vapour_rows, first_both, first_low, second, rank):
    rows, bins = x.shape
    lane = lax.broadcasted_iota(I32, (rows, bins), 1)
    place = lane & (SEGMENT - 1)
    one_lanes = jnp.where((place >= rank) & (place < 2 * rank), 1.0, 0.0).astype(F32)
    high, low = split(x)
    proj = jnp.dot(jnp.concatenate([high, low], 1), first_both[...], preferred_element_type=F32)
    proj = proj + jnp.dot(high, first_low[...], preferred_element_type=F32)
    left, right = proj[:, :bins], proj[:, bins:]
    taken = vapour_rows / (1.0 + vapour_rows * left)
    product = jnp.where(place == TAKE_LANE, taken, left * (right + one_lanes))
    product = jnp.where(lane < 3 * SEGMENT, product, 0.0)
    high, low = split(product)
    parts = jnp.where(lane < 2 * SEGMENT, high.astype(F32), low.astype(F32)).astype(BF16)
    rate = jnp.dot(parts, second[...], preferred_element_type=F32)
    return x + (rate[:, :bins] - x * rate[:, bins:])


def pack_kernel(
    haze_hbm,
    wind_ref,
    vapour_ref,
    uptake_ref,
    left_ref,
    right_ref,
    gain_ref,
    loss_ref,
    targets_hbm,
    upwind_hbm,
    packed_ref,
    top_ref,
    wind_top_ref,
    first_both,
    first_low,
    second,
    slot_ref,
    source_ref,
    haze_buf,
    columns,
    second_buf,
    window,
    upwind_window,
    used,
    haze_sems,
    window_sems,
):
    blocks, cells, bins = haze_buf.shape
    rank = left_ref.shape[0]
    group = 8
    rows = group * cells
    wide_count = lax.axis_size("wide")
    owner = lax.axis_index("wide")
    first = lax.axis_index("narrow") == 0
    start = owner * blocks
    base = pl.multiple_of((start // 128) * 128, 128)
    far_base = pl.multiple_of((start // 1024) * 1024, 1024)
    window_copies = [
        pltpu.make_async_copy(targets_hbm.at[:, pl.ds(base, 128)], window, window_sems.at[0]),
        pltpu.make_async_copy(
            upwind_hbm.at[pl.ds(far_base, 1024)], upwind_window, window_sems.at[1]
        ),
    ]
    for copy in window_copies:
        copy.start()
    copies = []
    for g in range(blocks // group):
        part = pl.ds(g * group, group)
        copy = pltpu.make_async_copy(haze_hbm.at[part], haze_buf.at[part], haze_sems.at[g])
        copy.start()
        copies.append(copy)
    packed_ref[...] = jnp.zeros_like(packed_ref)
    for t in range(used.shape[0]):
        used[t] = 0
    fill_weights(
        columns,
        second_buf,
        first_both,
        first_low,
        second,
        left_ref[...],
        right_ref[...],
        uptake_ref[...],
        gain_ref[...],
        loss_ref[...],
    )
    top_row = lax.broadcasted_iota(I32, (rows, bins), 0) % cells == 0
    wind = wind_ref[...]
    vapour = vapour_ref[...]
    wind_top_ref[...] = rows_of_lanes(wind_ref[0:1, :], bins)
    for copy in window_copies:
        copy.wait()
    block_bits = blocks.bit_length() - 1
    column_bits = COLUMNS.bit_length() - 1
    line_bits = (wide_count // COLUMNS).bit_length() - 1
    for g in range(blocks // group):
        copies[g].wait()
        x = haze_buf[g * group : (g + 1) * group].reshape(rows, bins)
        ids = range(g * group, (g + 1) * group)
        vapour_rows = jnp.concatenate([column_rows(vapour, b, cells, bins) for b in ids], 0)
        wind_rows = jnp.concatenate([column_rows(wind, b, cells, bins) for b in ids], 0)
        grown = grow(x, vapour_rows, first_both, first_low, second, rank)
        upwind = jnp.where(top_row, 0.0, pltpu.roll(grown, 1, 0))
        moved = grown - wind_rows * (grown - upwind)
        for j, b in enumerate(ids):
            at = j * cells
            target = window[0, start - base + b]
            rank_within = used[target]
            used[target] = rank_within + 1
            position = ((target & (COLUMNS - 1)) << line_bits) + (target >> column_bits)
            slot = position * 2 + rank_within
            slot_ref[b] = slot
            packed_ref[slot] = moved[at : at + cells, :]
            top_ref[b : b + 1, :] = moved[at : at + 1, :]
            source = upwind_window[start - far_base + b]
            relative = ((source >> block_bits) - owner + 1 + wide_count) & (wide_count - 1)
            far = (relative << block_bits) + (source & (blocks - 1))
            source_ref[b] = jnp.where(first, far, blocks + b)


def inflow_kernel(
    packed_in,
    top_ref,
    wind_top_ref,
    same_ref,
    low_ref,
    high_ref,
    first_both,
    first_low,
    second,
    slot_ref,
    source_ref,
    packed_hbm,
    near,
    inflow,
    rows_buf,
    sem,
    *,
    rank,
):
    blocks, bins = top_ref.shape
    near[0:blocks, :] = low_ref[...]
    near[blocks : 2 * blocks, :] = same_ref[...]
    near[2 * blocks :, :] = high_ref[...]
    for b in range(blocks):
        rows_buf[b : b + 1, :] = near[pl.ds(source_ref[b], 1), :]
    grown = grow(rows_buf[:, :bins], rows_buf[:, bins:], first_both, first_low, second, rank)
    inflow[...] = top_ref[...] + wind_top_ref[...] * grown
    for b in range(blocks):
        pltpu.make_async_copy(inflow.at[b], packed_hbm.at[slot_ref[b], 0], sem).start()
    pltpu.make_async_copy(inflow, packed_hbm.at[pl.ds(0, blocks), 0, :], sem).wait()


def vapour_kernel(haze_ref, vapour_ref, uptake_ref, vapour_out_ref):
    blocks, cells, bins = haze_ref.shape
    vapour = vapour_ref[...]
    weights = jnp.broadcast_to(uptake_ref[...] * (1.0 / bins), (bins, bins)).T
    lane = lax.broadcasted_iota(I32, (cells, blocks), 1)
    out = jnp.zeros((cells, blocks), F32)
    for g in range(0, blocks, 8):
        mean_take = precise_dot(haze_ref[g : g + 8].reshape(8 * cells, bins), weights)
        for j in range(8):
            part = mean_take[j * cells : (j + 1) * cells, :blocks]
            out = jnp.where(lane == g + j, part, out)
    vapour_out_ref[...] = vapour * (1.0 / (1.0 + vapour * out))


def whole(space=VMEM):
    return pl.BlockSpec(memory_space=space)


def cost(flops, moved):
    return pl.CostEstimate(flops=flops, bytes_accessed=moved, transcendentals=0)


def local(
    haze_bin_mass,
    wind_speed,
    vapour,
    uptake_rates,
    coag_left,
    coag_right,
    coag_gain,
    coag_loss,
    targets,
    upwind_blocks,
):
    wide_count = lax.axis_size("wide")
    narrow_count = lax.axis_size("narrow")
    blocks, cells, bins = haze_bin_mass.shape
    slots = 2 * wide_count
    vapour_t = vapour.T
    uptake_row = uptake_rates[None, :]
    rates = (uptake_row, coag_left.T, coag_right.T, coag_gain, coag_loss)
    rim = jnp.concatenate(
        [haze_bin_mass[:, cells - 1, :], jnp.broadcast_to(vapour[:, cells - 1 :], (blocks, bins))], 1
    )

    def passed(distance):
        route = [
            (
                w * narrow_count + n,
                ((w + distance) % wide_count) * narrow_count + (n + 1) % narrow_count,
            )
            for w in range(wide_count)
            for n in range(narrow_count)
        ]
        return lax.ppermute(rim, ("wide", "narrow"), route)

    same, low, high = passed(0), passed(1), passed(-1)

    def shape(*dims, kind=F32):
        return jax.ShapeDtypeStruct(dims, kind)

    packed_type = shape(slots, cells, bins)
    packed, top, wind_top, first_both, first_low, second, slot, source = pl.pallas_call(
        pack_kernel,
        out_shape=(
            packed_type,
            shape(blocks, bins),
            shape(blocks, bins),
            shape(2 * bins, 2 * bins, kind=BF16),
            shape(bins, 2 * bins, kind=BF16),
            shape(bins, 2 * bins, kind=BF16),
            shape(blocks, kind=I32),
            shape(blocks, kind=I32),
        ),
        in_specs=[whole(pl.ANY)] + [whole()] * 7 + [whole(pl.ANY)] * 2,
        out_specs=(whole(),) * 6 + (whole(pltpu.SMEM),) * 2,
        scratch_shapes=[
            pltpu.VMEM((blocks, cells, bins), F32),
            pltpu.VMEM((2 * bins, bins), F32),
            pltpu.VMEM((SEGMENT, 2 * bins), F32),
            pltpu.SMEM((1, 128), I32),
            pltpu.SMEM((1024,), I32),
            pltpu.SMEM((wide_count,), I32),
            pltpu.SemaphoreType.DMA((blocks // 8,)),
            pltpu.SemaphoreType.DMA((2,)),
        ],
        cost_estimate=cost(800000000, 4000000),
        compiler_params=pltpu.CompilerParams(vmem_limit_bytes=67043328),
    )(haze_bin_mass, wind_speed.T, vapour_t, *rates, targets.T, upwind_blocks)

    def fill_in(*refs):
        inflow_kernel(*refs, rank=coag_left.shape[1])

    packed = pl.pallas_call(
        fill_in,
        out_shape=packed_type,
        in_specs=[whole(pl.ANY)] + [whole()] * 8 + [whole(pltpu.SMEM)] * 2,
        out_specs=whole(pl.ANY),
        scratch_shapes=[
            pltpu.VMEM((3 * blocks, 2 * bins), F32),
            pltpu.VMEM((blocks, bins), F32),
            pltpu.VMEM((blocks, 2 * bins), F32),
            pltpu.SemaphoreType.DMA,
        ],
        input_output_aliases={0: 0},
        cost_estimate=cost(100000, 300000),
    )(packed, top, wind_top, same, low, high, first_both, first_low, second, slot, source)
    lines = wide_count // COLUMNS
    order = [line * COLUMNS + column for column in range(COLUMNS) for line in range(lines)]
    arrived = lax.all_to_all(
        packed, "wide", split_axis=0, concat_axis=0, tiled=True, axis_index_groups=[order]
    )
    arrived = arrived.reshape(COLUMNS, lines, 2, cells, bins)
    haze_output_slots = jnp.swapaxes(arrived, 0, 1).reshape(slots, cells, bins)
    vapour_out = pl.pallas_call(
        vapour_kernel,
        out_shape=shape(cells, blocks),
        in_specs=[whole()] * 3,
        out_specs=whole(),
        cost_estimate=cost(400000000, 1000000),
    )(haze_bin_mass, vapour_t, uptake_row)
    return (haze_output_slots, vapour_out.T)


def solution(mesh):
    in_specs = (
        P("wide", "narrow", None),
        P("wide", "narrow"),
        P("wide", "narrow"),
        P(),
        P(),
        P(),
        P(),
        P(),
        P(),
        P(),
    )
    out_specs = (P("wide", "narrow", None), P("wide", "narrow"))
    return jax.shard_map(local, mesh=mesh, in_specs=in_specs, out_specs=out_specs, check_vma=False)
```

```python
import jax
import jax.numpy as jnp
from jax import lax
from jax.experimental import pallas as pl
from jax.experimental.pallas import tpu as pltpu
from jax.sharding import PartitionSpec as P

HIGHEST = lax.Precision.HIGHEST
STEP_DT = 0.25
F32 = jnp.float32
BF16 = jnp.bfloat16
I32 = jnp.int32
VMEM = pltpu.VMEM
SEGMENT = 32
TAKE_LANE = 24
COLUMNS = 8


def precise_dot(a, b):
    return jnp.dot(a, b, precision=HIGHEST, preferred_element_type=F32)


def split(x):
    high = x.astype(BF16)
    return high, (x - high.astype(F32)).astype(BF16)


def column_rows(table, column, rows, lanes):
    return jnp.broadcast_to(table[:, column : column + 1], (rows, lanes))


def rows_of_lanes(row, lanes):
    count = row.shape[1]
    shape = (count, count)
    eye = lax.broadcasted_iota(I32, shape, 0) == lax.broadcasted_iota(I32, shape, 1)
    spread = jnp.where(eye, jnp.broadcast_to(row, shape), 0.0)
    return precise_dot(spread, jnp.ones((count, lanes), F32))


def fill_weights(columns, second, first_both, first_low, second_ref, left, right, uptake, gain, loss):
    rank, bins = left.shape
    columns[...] = jnp.zeros_like(columns)
    for at in range(0, 3 * SEGMENT, SEGMENT):
        columns[at : at + rank, :] = left
        columns[at + rank : at + 2 * rank, :] = left
        columns[at + TAKE_LANE : at + TAKE_LANE + 1, :] = uptake * (1.0 / bins)
        columns[bins + at : bins + at + rank, :] = right
    for k in range(0, 2 * bins, bins):
        high, low = split(columns[k : k + bins, :].T)
        first_both[0:bins, k : k + bins] = high
        first_both[bins:, k : k + bins] = high
        first_low[:, k : k + bins] = low
    second[...] = jnp.zeros_like(second)
    second[0:rank, 0:bins] = STEP_DT * gain
    second[rank : 2 * rank, bins:] = STEP_DT * loss
    second[TAKE_LANE : TAKE_LANE + 1, bins:] = -uptake
    high, low = split(second[...])
    second_ref[0:SEGMENT, :] = high
    second_ref[SEGMENT : 2 * SEGMENT, :] = low
    second_ref[2 * SEGMENT : 3 * SEGMENT, :] = high
    second_ref[3 * SEGMENT :, :] = jnp.zeros_like(high)


def grow(x, vapour_rows, first_both, first_low, second, rank):
    rows, bins = x.shape
    lane = lax.broadcasted_iota(I32, (rows, bins), 1)
    place = lane & (SEGMENT - 1)
    one_lanes = jnp.where((place >= rank) & (place < 2 * rank), 1.0, 0.0).astype(F32)
    high, low = split(x)
    proj = jnp.dot(jnp.concatenate([high, low], 1), first_both[...], preferred_element_type=F32)
    proj = proj + jnp.dot(high, first_low[...], preferred_element_type=F32)
    left, right = proj[:, :bins], proj[:, bins:]
    taken = vapour_rows / (1.0 + vapour_rows * left)
    product = jnp.where(place == TAKE_LANE, taken, left * (right + one_lanes))
    product = jnp.where(lane < 3 * SEGMENT, product, 0.0)
    high, low = split(product)
    parts = jnp.where(lane < 2 * SEGMENT, high.astype(F32), low.astype(F32)).astype(BF16)
    rate = jnp.dot(parts, second[...], preferred_element_type=F32)
    return x + (rate[:, :bins] - x * rate[:, bins:])


def rim_kernel(
    haze_hbm,
    vapour_ref,
    uptake_ref,
    left_ref,
    right_ref,
    gain_ref,
    loss_ref,
    rim_ref,
    rows_buf,
    columns,
    second_buf,
    first_both,
    first_low,
    second,
    sem,
):
    cells = haze_hbm.shape[1]
    copy = pltpu.make_async_copy(haze_hbm.at[:, cells - 1, :], rows_buf, sem)
    copy.start()
    fill_weights(
        columns,
        second_buf,
        first_both,
        first_low,
        second,
        left_ref[...],
        right_ref[...],
        uptake_ref[...],
        gain_ref[...],
        loss_ref[...],
    )
    vapour_rows = rows_of_lanes(vapour_ref[cells - 1 : cells, :], rows_buf.shape[1])
    copy.wait()
    rim_ref[...] = grow(
        rows_buf[...], vapour_rows, first_both, first_low, second, left_ref.shape[0]
    )


def pack_kernel(
    haze_hbm,
    wind_ref,
    vapour_ref,
    uptake_ref,
    left_ref,
    right_ref,
    gain_ref,
    loss_ref,
    targets_hbm,
    upwind_hbm,
    packed_ref,
    top_ref,
    wind_top_ref,
    slot_ref,
    source_ref,
    haze_buf,
    columns,
    second_buf,
    first_both,
    first_low,
    second,
    window,
    upwind_window,
    used,
    haze_sems,
    window_sems,
):
    blocks, cells, bins = haze_buf.shape
    rank = left_ref.shape[0]
    group = 8
    rows = group * cells
    wide_count = lax.axis_size("wide")
    owner = lax.axis_index("wide")
    first = lax.axis_index("narrow") == 0
    start = owner * blocks
    base = pl.multiple_of((start // 128) * 128, 128)
    far_base = pl.multiple_of((start // 1024) * 1024, 1024)
    window_copies = [
        pltpu.make_async_copy(targets_hbm.at[:, pl.ds(base, 128)], window, window_sems.at[0]),
        pltpu.make_async_copy(
            upwind_hbm.at[pl.ds(far_base, 1024)], upwind_window, window_sems.at[1]
        ),
    ]
    for copy in window_copies:
        copy.start()
    copies = []
    for g in range(blocks // group):
        part = pl.ds(g * group, group)
        copy = pltpu.make_async_copy(haze_hbm.at[part], haze_buf.at[part], haze_sems.at[g])
        copy.start()
        copies.append(copy)
    packed_ref[...] = jnp.zeros_like(packed_ref)
    for t in range(used.shape[0]):
        used[t] = 0
    fill_weights(
        columns,
        second_buf,
        first_both,
        first_low,
        second,
        left_ref[...],
        right_ref[...],
        uptake_ref[...],
        gain_ref[...],
        loss_ref[...],
    )
    top_row = lax.broadcasted_iota(I32, (rows, bins), 0) % cells == 0
    wind = wind_ref[...]
    vapour = vapour_ref[...]
    wind_top_ref[...] = rows_of_lanes(wind_ref[0:1, :], bins)
    for copy in window_copies + copies:
        copy.wait()
    block_bits = blocks.bit_length() - 1
    column_bits = COLUMNS.bit_length() - 1
    line_bits = (wide_count // COLUMNS).bit_length() - 1
    for g in range(blocks // group):
        x = haze_buf[g * group : (g + 1) * group].reshape(rows, bins)
        ids = range(g * group, (g + 1) * group)
        vapour_rows = jnp.concatenate([column_rows(vapour, b, cells, bins) for b in ids], 0)
        wind_rows = jnp.concatenate([column_rows(wind, b, cells, bins) for b in ids], 0)
        grown = grow(x, vapour_rows, first_both, first_low, second, rank)
        upwind = jnp.where(top_row, 0.0, pltpu.roll(grown, 1, 0))
        moved = grown - wind_rows * (grown - upwind)
        for j, b in enumerate(ids):
            at = j * cells
            target = window[0, start - base + b]
            rank_within = used[target]
            used[target] = rank_within + 1
            position = ((target & (COLUMNS - 1)) << line_bits) + (target >> column_bits)
            slot = position * 2 + rank_within
            slot_ref[b] = slot
            packed_ref[slot] = moved[at : at + cells, :]
            top_ref[b : b + 1, :] = moved[at : at + 1, :]
            source = upwind_window[start - far_base + b]
            relative = ((source >> block_bits) - owner + 1 + wide_count) & (wide_count - 1)
            far = (relative << block_bits) + (source & (blocks - 1))
            source_ref[b] = jnp.where(first, far, blocks + b)


def inflow_kernel(
    packed_in,
    top_ref,
    wind_top_ref,
    same_ref,
    low_ref,
    high_ref,
    slot_ref,
    source_ref,
    packed_hbm,
    near,
    inflow,
    sem,
):
    blocks, bins = top_ref.shape
    near[0:blocks, :] = low_ref[...]
    near[blocks : 2 * blocks, :] = same_ref[...]
    near[2 * blocks :, :] = high_ref[...]
    for b in range(blocks):
        inflow[b : b + 1, :] = near[pl.ds(source_ref[b], 1), :]
    inflow[...] = top_ref[...] + wind_top_ref[...] * inflow[...]
    for b in range(blocks):
        pltpu.make_async_copy(inflow.at[b], packed_hbm.at[slot_ref[b], 0], sem).start()
    pltpu.make_async_copy(inflow, packed_hbm.at[pl.ds(0, blocks), 0, :], sem).wait()


def vapour_kernel(haze_ref, vapour_ref, uptake_ref, vapour_out_ref):
    blocks, cells, bins = haze_ref.shape
    vapour = vapour_ref[...]
    weights = jnp.broadcast_to(uptake_ref[...] * (1.0 / bins), (bins, bins)).T
    lane = lax.broadcasted_iota(I32, (cells, blocks), 1)
    out = jnp.zeros((cells, blocks), F32)
    for g in range(0, blocks, 8):
        mean_take = precise_dot(haze_ref[g : g + 8].reshape(8 * cells, bins), weights)
        for j in range(8):
            part = mean_take[j * cells : (j + 1) * cells, :blocks]
            out = jnp.where(lane == g + j, part, out)
    vapour_out_ref[...] = vapour * (1.0 / (1.0 + vapour * out))


def whole(space=VMEM):
    return pl.BlockSpec(memory_space=space)


def cost(flops, moved):
    return pl.CostEstimate(flops=flops, bytes_accessed=moved, transcendentals=0)


def local(
    haze_bin_mass,
    wind_speed,
    vapour,
    uptake_rates,
    coag_left,
    coag_right,
    coag_gain,
    coag_loss,
    targets,
    upwind_blocks,
):
    wide_count = lax.axis_size("wide")
    narrow_count = lax.axis_size("narrow")
    blocks, cells, bins = haze_bin_mass.shape
    slots = 2 * wide_count
    vapour_t = vapour.T
    uptake_row = uptake_rates[None, :]
    rates = (uptake_row, coag_left.T, coag_right.T, coag_gain, coag_loss)
    def shape(*dims, kind=F32):
        return jax.ShapeDtypeStruct(dims, kind)

    weight_scratch = [
        pltpu.VMEM((2 * bins, bins), F32),
        pltpu.VMEM((SEGMENT, 2 * bins), F32),
        pltpu.VMEM((2 * bins, 2 * bins), BF16),
        pltpu.VMEM((bins, 2 * bins), BF16),
        pltpu.VMEM((bins, 2 * bins), BF16),
    ]
    rows_type = shape(blocks, bins)
    rim = pl.pallas_call(
        rim_kernel,
        out_shape=rows_type,
        in_specs=[whole(pl.ANY)] + [whole()] * 6,
        out_specs=whole(),
        scratch_shapes=[
            pltpu.VMEM((blocks, bins), F32),
            *weight_scratch,
            pltpu.SemaphoreType.DMA,
        ],
        cost_estimate=cost(10000000, 100000),
    )(haze_bin_mass, vapour_t, *rates)
    last = narrow_count - 1

    def flat(w, n):
        return (w % wide_count) * narrow_count + n % narrow_count

    def passed(distance):
        if distance == 0:
            route = [
                (flat(w, n), flat(w, n + 1)) for w in range(wide_count) for n in range(narrow_count)
            ]
        else:
            route = [(flat(w, last), flat(w + distance, 0)) for w in range(wide_count)]
            route += [(flat(w, n), flat(w, n)) for w in range(wide_count) for n in range(1, last)]
        return lax.ppermute(rim, ("wide", "narrow"), route)

    same, low, high = passed(0), passed(1), passed(-1)
    packed_type = shape(slots, cells, bins)
    packed, top, wind_top, slot, source = pl.pallas_call(
        pack_kernel,
        out_shape=(packed_type, rows_type, rows_type, shape(blocks, kind=I32), shape(blocks, kind=I32)),
        in_specs=[whole(pl.ANY)] + [whole()] * 7 + [whole(pl.ANY)] * 2,
        out_specs=(whole(),) * 3 + (whole(pltpu.SMEM),) * 2,
        scratch_shapes=[
            pltpu.VMEM((blocks, cells, bins), F32),
            *weight_scratch,
            pltpu.SMEM((1, 128), I32),
            pltpu.SMEM((1024,), I32),
            pltpu.SMEM((wide_count,), I32),
            pltpu.SemaphoreType.DMA((blocks // 8,)),
            pltpu.SemaphoreType.DMA((2,)),
        ],
        cost_estimate=cost(800000000, 4000000),
        compiler_params=pltpu.CompilerParams(vmem_limit_bytes=67043328),
    )(haze_bin_mass, wind_speed.T, vapour_t, *rates, targets.T, upwind_blocks)
    packed = pl.pallas_call(
        inflow_kernel,
        out_shape=packed_type,
        in_specs=[whole(pl.ANY)] + [whole()] * 5 + [whole(pltpu.SMEM)] * 2,
        out_specs=whole(pl.ANY),
        scratch_shapes=[
            pltpu.VMEM((3 * blocks, bins), F32),
            pltpu.VMEM((blocks, bins), F32),
            pltpu.SemaphoreType.DMA,
        ],
        input_output_aliases={0: 0},
        cost_estimate=cost(100000, 300000),
    )(packed, top, wind_top, same, low, high, slot, source)
    lines = wide_count // COLUMNS
    order = [line * COLUMNS + column for column in range(COLUMNS) for line in range(lines)]
    arrived = lax.all_to_all(
        packed, "wide", split_axis=0, concat_axis=0, tiled=True, axis_index_groups=[order]
    )
    arrived = arrived.reshape(COLUMNS, lines, 2, cells, bins)
    haze_output_slots = jnp.swapaxes(arrived, 0, 1).reshape(slots, cells, bins)
    vapour_out = pl.pallas_call(
        vapour_kernel,
        out_shape=shape(cells, blocks),
        in_specs=[whole()] * 3,
        out_specs=whole(),
        cost_estimate=cost(400000000, 1000000),
    )(haze_bin_mass, vapour_t, uptake_row)
    return (haze_output_slots, vapour_out.T)


def solution(mesh):
    in_specs = (
        P("wide", "narrow", None),
        P("wide", "narrow"),
        P("wide", "narrow"),
        P(),
        P(),
        P(),
        P(),
        P(),
        P(),
        P(),
    )
    out_specs = (P("wide", "narrow", None), P("wide", "narrow"))
    return jax.shard_map(local, mesh=mesh, in_specs=in_specs, out_specs=out_specs, check_vma=False)
```

```python
import jax
import jax.numpy as jnp
from jax import lax
from jax.experimental import pallas as pl
from jax.experimental.pallas import tpu as pltpu
from jax.sharding import PartitionSpec as P

HIGHEST = lax.Precision.HIGHEST
STEP_DT = 0.25
F32 = jnp.float32
BF16 = jnp.bfloat16
I32 = jnp.int32
VMEM = pltpu.VMEM
SEGMENT = 32
TAKE_LANE = 24
COLUMNS = 8


def precise_dot(a, b):
    return jnp.dot(a, b, precision=HIGHEST, preferred_element_type=F32)


def split(x):
    high = x.astype(BF16)
    return high, (x - high.astype(F32)).astype(BF16)


def column_rows(table, column, rows, lanes):
    return jnp.broadcast_to(table[:, column : column + 1], (rows, lanes))


def rows_of_lanes(row, lanes):
    count = row.shape[1]
    shape = (count, count)
    eye = lax.broadcasted_iota(I32, shape, 0) == lax.broadcasted_iota(I32, shape, 1)
    spread = jnp.where(eye, jnp.broadcast_to(row, shape), 0.0)
    return precise_dot(spread, jnp.ones((count, lanes), F32))


def fill_weights(columns, second, first_both, first_low, second_ref, left, right, uptake, gain, loss):
    rank, bins = left.shape
    columns[...] = jnp.zeros_like(columns)
    for at in range(0, 3 * SEGMENT, SEGMENT):
        columns[at : at + rank, :] = left
        columns[at + rank : at + 2 * rank, :] = left
        columns[at + TAKE_LANE : at + TAKE_LANE + 1, :] = uptake * (1.0 / bins)
        columns[bins + at : bins + at + rank, :] = right
    for k in range(0, 2 * bins, bins):
        high, low = split(columns[k : k + bins, :].T)
        first_both[0:bins, k : k + bins] = high
        first_both[bins:, k : k + bins] = high
        first_low[:, k : k + bins] = low
    second[...] = jnp.zeros_like(second)
    second[0:rank, 0:bins] = STEP_DT * gain
    second[rank : 2 * rank, bins:] = STEP_DT * loss
    second[TAKE_LANE : TAKE_LANE + 1, bins:] = -uptake
    high, low = split(second[...])
    second_ref[0:SEGMENT, :] = high
    second_ref[SEGMENT : 2 * SEGMENT, :] = low
    second_ref[2 * SEGMENT : 3 * SEGMENT, :] = high
    second_ref[3 * SEGMENT :, :] = jnp.zeros_like(high)


def grow(x, vapour_rows, first_both, first_low, second, rank):
    rows, bins = x.shape
    lane = lax.broadcasted_iota(I32, (rows, bins), 1)
    place = lane & (SEGMENT - 1)
    one_lanes = jnp.where((place >= rank) & (place < 2 * rank), 1.0, 0.0).astype(F32)
    high, low = split(x)
    proj = jnp.dot(jnp.concatenate([high, low], 1), first_both[...], preferred_element_type=F32)
    proj = proj + jnp.dot(high, first_low[...], preferred_element_type=F32)
    left, right = proj[:, :bins], proj[:, bins:]
    taken = vapour_rows / (1.0 + vapour_rows * left)
    product = jnp.where(place == TAKE_LANE, taken, left * (right + one_lanes))
    product = jnp.where(lane < 3 * SEGMENT, product, 0.0)
    high, low = split(product)
    parts = jnp.where(lane < 2 * SEGMENT, high.astype(F32), low.astype(F32)).astype(BF16)
    rate = jnp.dot(parts, second[...], preferred_element_type=F32)
    return x + (rate[:, :bins] - x * rate[:, bins:])


def rim_kernel(
    haze_hbm,
    vapour_ref,
    uptake_ref,
    left_ref,
    right_ref,
    gain_ref,
    loss_ref,
    rim_ref,
    rows_buf,
    columns,
    second_buf,
    first_both,
    first_low,
    second,
    sem,
):
    cells = haze_hbm.shape[1]
    copy = pltpu.make_async_copy(haze_hbm.at[:, cells - 1, :], rows_buf, sem)
    copy.start()
    fill_weights(
        columns,
        second_buf,
        first_both,
        first_low,
        second,
        left_ref[...],
        right_ref[...],
        uptake_ref[...],
        gain_ref[...],
        loss_ref[...],
    )
    vapour_rows = rows_of_lanes(vapour_ref[cells - 1 : cells, :], rows_buf.shape[1])
    copy.wait()
    rim_ref[...] = grow(
        rows_buf[...], vapour_rows, first_both, first_low, second, left_ref.shape[0]
    )


def pack_kernel(
    haze_hbm,
    wind_ref,
    vapour_ref,
    uptake_ref,
    left_ref,
    right_ref,
    gain_ref,
    loss_ref,
    upwind_ref,
    targets_hbm,
    packed_ref,
    top_ref,
    wind_top_ref,
    slot_ref,
    source_ref,
    haze_buf,
    columns,
    second_buf,
    first_both,
    first_low,
    second,
    window,
    used,
    haze_sems,
    window_sem,
):
    blocks, cells, bins = haze_buf.shape
    rank = left_ref.shape[0]
    group = 64
    rows = group * cells
    wide_count = lax.axis_size("wide")
    owner = lax.axis_index("wide")
    first = lax.axis_index("narrow") == 0
    start = owner * blocks
    base = pl.multiple_of((start // 128) * 128, 128)
    window_copy = pltpu.make_async_copy(
        targets_hbm.at[:, pl.ds(base, 128)], window, window_sem
    )
    window_copy.start()
    copies = []
    for g in range(blocks // group):
        part = pl.ds(g * group, group)
        copy = pltpu.make_async_copy(haze_hbm.at[part], haze_buf.at[part], haze_sems.at[g])
        copy.start()
        copies.append(copy)
    packed_ref[...] = jnp.zeros_like(packed_ref)
    lines = wide_count // COLUMNS
    odd = lax.axis_index("narrow") & 1
    for t in range(wide_count):
        used[t] = jnp.where(odd == 1, 2 * t, 2 * ((t % COLUMNS) * lines + t // COLUMNS))
    fill_weights(
        columns,
        second_buf,
        first_both,
        first_low,
        second,
        left_ref[...],
        right_ref[...],
        uptake_ref[...],
        gain_ref[...],
        loss_ref[...],
    )
    top_row = lax.broadcasted_iota(I32, (rows, bins), 0) % cells == 0
    wind = wind_ref[...]
    vapour = vapour_ref[...]
    wind_top_ref[...] = rows_of_lanes(wind_ref[0:1, :], bins)
    upwind = upwind_ref[pl.ds(start // 128, 1), :]
    block_bits = blocks.bit_length() - 1
    relative = ((upwind >> block_bits) - owner + 1 + wide_count) & (wide_count - 1)
    far = (relative << block_bits) + (upwind & (blocks - 1))
    near = blocks + (lax.broadcasted_iota(I32, far.shape, 1) & (blocks - 1))
    source_ref[...] = jnp.where(first, far, near)
    for copy in [window_copy] + copies:
        copy.wait()
    for g in range(blocks // group):
        x = haze_buf[g * group : (g + 1) * group].reshape(rows, bins)
        ids = range(g * group, (g + 1) * group)
        vapour_rows = jnp.concatenate([column_rows(vapour, b, cells, bins) for b in ids], 0)
        wind_rows = jnp.concatenate([column_rows(wind, b, cells, bins) for b in ids], 0)
        grown = grow(x, vapour_rows, first_both, first_low, second, rank)
        upwind = jnp.where(top_row, 0.0, pltpu.roll(grown, 1, 0))
        moved = grown - wind_rows * (grown - upwind)
        for j, b in enumerate(ids):
            at = j * cells
            target = window[0, start - base + b]
            slot = used[target]
            used[target] = slot + 1
            slot_ref[b] = slot
            packed_ref[slot] = moved[at : at + cells, :]
            top_ref[b : b + 1, :] = moved[at : at + 1, :]


def inflow_kernel(
    packed_in,
    top_ref,
    wind_top_ref,
    same_ref,
    low_ref,
    high_ref,
    slot_ref,
    source_ref,
    packed_hbm,
    near,
    inflow,
    sem,
):
    blocks, bins = top_ref.shape
    near[0:blocks, :] = low_ref[...]
    near[blocks : 2 * blocks, :] = same_ref[...]
    near[2 * blocks :, :] = high_ref[...]
    offset = (lax.axis_index("wide") * blocks) % 128
    for b in range(blocks):
        inflow[b : b + 1, :] = near[pl.ds(source_ref[0, offset + b], 1), :]
    inflow[...] = top_ref[...] + wind_top_ref[...] * inflow[...]
    for b in range(blocks):
        pltpu.make_async_copy(inflow.at[b], packed_hbm.at[slot_ref[b], 0], sem).start()
    pltpu.make_async_copy(inflow, packed_hbm.at[pl.ds(0, blocks), 0, :], sem).wait()


def place_kernel(arrived_ref, out_hbm, sem):
    wide_count = lax.axis_size("wide")
    lines = wide_count // COLUMNS
    odd = lax.axis_index("narrow") & 1
    for p in range(wide_count):
        source = jnp.where(odd == 1, p, (p % lines) * COLUMNS + p // lines)
        pltpu.make_async_copy(
            arrived_ref.at[pl.ds(2 * p, 2)], out_hbm.at[pl.ds(2 * source, 2)], sem
        ).start()
    pltpu.make_async_copy(arrived_ref, out_hbm, sem).wait()


def vapour_kernel(haze_ref, vapour_ref, uptake_ref, vapour_out_ref):
    blocks, cells, bins = haze_ref.shape
    vapour = vapour_ref[...]
    weights = jnp.broadcast_to(uptake_ref[...] * (1.0 / bins), (bins, bins)).T
    lane = lax.broadcasted_iota(I32, (cells, blocks), 1)
    out = jnp.zeros((cells, blocks), F32)
    for g in range(0, blocks, 8):
        mean_take = precise_dot(haze_ref[g : g + 8].reshape(8 * cells, bins), weights)
        for j in range(8):
            part = mean_take[j * cells : (j + 1) * cells, :blocks]
            out = jnp.where(lane == g + j, part, out)
    vapour_out_ref[...] = vapour * (1.0 / (1.0 + vapour * out))


def whole(space=VMEM):
    return pl.BlockSpec(memory_space=space)


def cost(flops, moved):
    return pl.CostEstimate(flops=flops, bytes_accessed=moved, transcendentals=0)


def local(
    haze_bin_mass,
    wind_speed,
    vapour,
    uptake_rates,
    coag_left,
    coag_right,
    coag_gain,
    coag_loss,
    targets,
    upwind_blocks,
):
    wide_count = lax.axis_size("wide")
    narrow_count = lax.axis_size("narrow")
    blocks, cells, bins = haze_bin_mass.shape
    slots = 2 * wide_count
    vapour_t = vapour.T
    uptake_row = uptake_rates[None, :]
    rates = (uptake_row, coag_left.T, coag_right.T, coag_gain, coag_loss)
    def shape(*dims, kind=F32):
        return jax.ShapeDtypeStruct(dims, kind)

    weight_scratch = [
        pltpu.VMEM((2 * bins, bins), F32),
        pltpu.VMEM((SEGMENT, 2 * bins), F32),
        pltpu.VMEM((2 * bins, 2 * bins), BF16),
        pltpu.VMEM((bins, 2 * bins), BF16),
        pltpu.VMEM((bins, 2 * bins), BF16),
    ]
    rows_type = shape(blocks, bins)
    rim = pl.pallas_call(
        rim_kernel,
        out_shape=rows_type,
        in_specs=[whole(pl.ANY)] + [whole()] * 6,
        out_specs=whole(),
        scratch_shapes=[
            pltpu.VMEM((blocks, bins), F32),
            *weight_scratch,
            pltpu.SemaphoreType.DMA,
        ],
        cost_estimate=cost(10000000, 100000),
    )(haze_bin_mass, vapour_t, *rates)
    both = ("wide", "narrow")
    last = narrow_count - 1

    def flat(w, n):
        return (w % wide_count) * narrow_count + n % narrow_count

    def passed(distance):
        if distance == 0:
            route = [
                (flat(w, n), flat(w, n + 1)) for w in range(wide_count) for n in range(narrow_count)
            ]
        else:
            route = [(flat(w, last), flat(w + distance, 0)) for w in range(wide_count)]
        return lax.ppermute(rim, both, route)

    same, low, high = passed(0), passed(1), passed(-1)
    packed_type = shape(slots, cells, bins)
    packed, top, wind_top, slot, source = pl.pallas_call(
        pack_kernel,
        out_shape=(packed_type, rows_type, rows_type, shape(blocks, kind=I32), shape(1, 128, kind=I32)),
        in_specs=[whole(pl.ANY)] + [whole()] * 8 + [whole(pl.ANY)],
        out_specs=(whole(),) * 3 + (whole(pltpu.SMEM), whole()),
        scratch_shapes=[
            pltpu.VMEM((blocks, cells, bins), F32),
            *weight_scratch,
            pltpu.SMEM((1, 128), I32),
            pltpu.SMEM((wide_count,), I32),
            pltpu.SemaphoreType.DMA((blocks // 64,)),
            pltpu.SemaphoreType.DMA,
        ],
        cost_estimate=cost(800000000, 4000000),
        compiler_params=pltpu.CompilerParams(vmem_limit_bytes=67043328),
    )(haze_bin_mass, wind_speed.T, vapour_t, *rates, upwind_blocks.reshape(-1, 128), targets.T)
    packed = pl.pallas_call(
        inflow_kernel,
        out_shape=packed_type,
        in_specs=[whole(pl.ANY)] + [whole()] * 5 + [whole(pltpu.SMEM)] * 2,
        out_specs=whole(pl.ANY),
        scratch_shapes=[
            pltpu.VMEM((3 * blocks, bins), F32),
            pltpu.VMEM((blocks, bins), F32),
            pltpu.SemaphoreType.DMA,
        ],
        input_output_aliases={0: 0},
        cost_estimate=cost(100000, 300000),
    )(packed, top, wind_top, same, low, high, slot, source)
    lines = wide_count // COLUMNS
    order = [line * COLUMNS + column for column in range(COLUMNS) for line in range(lines)]
    groups = [
        [w * narrow_count + n for w in (range(wide_count) if n % 2 else order)]
        for n in range(narrow_count)
    ]
    arrived = lax.all_to_all(
        packed, both, split_axis=0, concat_axis=0, tiled=True, axis_index_groups=groups
    )
    haze_output_slots = pl.pallas_call(
        place_kernel,
        out_shape=packed_type,
        in_specs=[whole(pl.ANY)],
        out_specs=whole(pl.ANY),
        scratch_shapes=[pltpu.SemaphoreType.DMA],
        cost_estimate=cost(0, 4000000),
        compiler_params=pltpu.CompilerParams(vmem_limit_bytes=1048576),
    )(arrived)
    vapour_out = pl.pallas_call(
        vapour_kernel,
        out_shape=shape(cells, blocks),
        in_specs=[whole()] * 3,
        out_specs=whole(),
        cost_estimate=cost(400000000, 1000000),
    )(haze_bin_mass, vapour_t, uptake_row)
    return (haze_output_slots, vapour_out.T)


def solution(mesh):
    in_specs = (
        P("wide", "narrow", None),
        P("wide", "narrow"),
        P("wide", "narrow"),
        P(),
        P(),
        P(),
        P(),
        P(),
        P(),
        P(),
    )
    out_specs = (P("wide", "narrow", None), P("wide", "narrow"))
    return jax.shard_map(local, mesh=mesh, in_specs=in_specs, out_specs=out_specs, check_vma=False)
```

```python
import jax
import jax.numpy as jnp
from jax import lax
from jax.experimental import pallas as pl
from jax.experimental.pallas import tpu as pltpu
from jax.sharding import PartitionSpec as P

HIGHEST = lax.Precision.HIGHEST
STEP_DT = 0.25
F32 = jnp.float32
BF16 = jnp.bfloat16
I32 = jnp.int32
VMEM = pltpu.VMEM
SEGMENT = 32
TAKE_LANE = 24
COLUMNS = 8


def precise_dot(a, b):
    return jnp.dot(a, b, precision=HIGHEST, preferred_element_type=F32)


def split(x):
    high = x.astype(BF16)
    return high, (x - high.astype(F32)).astype(BF16)


def column_rows(table, column, rows, lanes):
    return jnp.broadcast_to(table[:, column : column + 1], (rows, lanes))


def rows_of_lanes(row, lanes):
    count = row.shape[1]
    shape = (count, count)
    eye = lax.broadcasted_iota(I32, shape, 0) == lax.broadcasted_iota(I32, shape, 1)
    spread = jnp.where(eye, jnp.broadcast_to(row, shape), 0.0)
    return precise_dot(spread, jnp.ones((count, lanes), F32))


def fill_weights(columns, second, first_both, first_low, second_ref, left, right, uptake, gain, loss):
    rank, bins = left.shape
    columns[...] = jnp.zeros_like(columns)
    for at in range(0, 3 * SEGMENT, SEGMENT):
        columns[at : at + rank, :] = left
        columns[at + rank : at + 2 * rank, :] = left
        columns[at + TAKE_LANE : at + TAKE_LANE + 1, :] = uptake * (1.0 / bins)
        columns[bins + at : bins + at + rank, :] = right
    for k in range(0, 2 * bins, bins):
        high, low = split(columns[k : k + bins, :].T)
        first_both[0:bins, k : k + bins] = high
        first_both[bins:, k : k + bins] = high
        first_low[:, k : k + bins] = low
    second[...] = jnp.zeros_like(second)
    second[0:rank, 0:bins] = STEP_DT * gain
    second[rank : 2 * rank, bins:] = STEP_DT * loss
    second[TAKE_LANE : TAKE_LANE + 1, bins:] = -uptake
    high, low = split(second[...])
    second_ref[0:SEGMENT, :] = high
    second_ref[SEGMENT : 2 * SEGMENT, :] = low
    second_ref[2 * SEGMENT : 3 * SEGMENT, :] = high
    second_ref[3 * SEGMENT :, :] = jnp.zeros_like(high)


def grow(x, vapour_rows, first_both, first_low, second, rank):
    rows, bins = x.shape
    lane = lax.broadcasted_iota(I32, (rows, bins), 1)
    place = lane & (SEGMENT - 1)
    one_lanes = jnp.where((place >= rank) & (place < 2 * rank), 1.0, 0.0).astype(F32)
    high, low = split(x)
    proj = jnp.dot(jnp.concatenate([high, low], 1), first_both[...], preferred_element_type=F32)
    proj = proj + jnp.dot(high, first_low[...], preferred_element_type=F32)
    left, right = proj[:, :bins], proj[:, bins:]
    taken = vapour_rows / (1.0 + vapour_rows * left)
    product = jnp.where(place == TAKE_LANE, taken, left * (right + one_lanes))
    product = jnp.where(lane < 3 * SEGMENT, product, 0.0)
    high, low = split(product)
    parts = jnp.where(lane < 2 * SEGMENT, high.astype(F32), low.astype(F32)).astype(BF16)
    rate = jnp.dot(parts, second[...], preferred_element_type=F32)
    return x + (rate[:, :bins] - x * rate[:, bins:])


def fetched(sources, targets, sems):
    copies = []
    for i, (source, target) in enumerate(zip(sources, targets, strict=True)):
        copy = pltpu.make_async_copy(source, target, sems.at[i])
        copy.start()
        copies.append(copy)
    return copies


def rim_kernel(
    haze_hbm,
    vapour_hbm,
    uptake_hbm,
    left_hbm,
    right_hbm,
    gain_hbm,
    loss_hbm,
    rim_ref,
    rows_buf,
    vapour_ref,
    uptake_ref,
    left_ref,
    right_ref,
    gain_ref,
    loss_ref,
    columns,
    second_buf,
    first_both,
    first_low,
    second,
    sem,
    small_sems,
):
    cells = haze_hbm.shape[1]
    copy = pltpu.make_async_copy(haze_hbm.at[:, cells - 1, :], rows_buf, sem)
    copy.start()
    small = fetched(
        (vapour_hbm, uptake_hbm, left_hbm, right_hbm, gain_hbm, loss_hbm),
        (vapour_ref, uptake_ref, left_ref, right_ref, gain_ref, loss_ref),
        small_sems,
    )
    for part in small:
        part.wait()
    fill_weights(
        columns,
        second_buf,
        first_both,
        first_low,
        second,
        left_ref[...],
        right_ref[...],
        uptake_ref[...],
        gain_ref[...],
        loss_ref[...],
    )
    vapour_rows = rows_of_lanes(vapour_ref[cells - 1 : cells, :], rows_buf.shape[1])
    copy.wait()
    rim_ref[...] = grow(
        rows_buf[...], vapour_rows, first_both, first_low, second, left_ref.shape[0]
    )


def pack_kernel(
    haze_hbm,
    wind_hbm,
    vapour_hbm,
    uptake_hbm,
    left_hbm,
    right_hbm,
    gain_hbm,
    loss_hbm,
    upwind_hbm,
    targets_hbm,
    packed_ref,
    top_ref,
    wind_top_ref,
    slot_ref,
    source_ref,
    haze_buf,
    wind_ref,
    vapour_ref,
    uptake_ref,
    left_ref,
    right_ref,
    gain_ref,
    loss_ref,
    upwind_ref,
    columns,
    second_buf,
    first_both,
    first_low,
    second,
    window,
    used,
    haze_sems,
    window_sem,
    small_sems,
):
    blocks, cells, bins = haze_buf.shape
    rank = left_ref.shape[0]
    group = 64
    rows = group * cells
    wide_count = lax.axis_size("wide")
    owner = lax.axis_index("wide")
    first = lax.axis_index("narrow") == 0
    start = owner * blocks
    base = pl.multiple_of((start // 128) * 128, 128)
    window_copy = pltpu.make_async_copy(
        targets_hbm.at[:, pl.ds(base, 128)], window, window_sem
    )
    window_copy.start()
    copies = []
    for g in range(blocks // group):
        part = pl.ds(g * group, group)
        copy = pltpu.make_async_copy(haze_hbm.at[part], haze_buf.at[part], haze_sems.at[g])
        copy.start()
        copies.append(copy)
    small = fetched(
        (wind_hbm, vapour_hbm, uptake_hbm, left_hbm, right_hbm, gain_hbm, loss_hbm, upwind_hbm),
        (wind_ref, vapour_ref, uptake_ref, left_ref, right_ref, gain_ref, loss_ref, upwind_ref),
        small_sems,
    )
    packed_ref[...] = jnp.zeros_like(packed_ref)
    lines = wide_count // COLUMNS
    odd = lax.axis_index("narrow") & 1
    for t in range(wide_count):
        used[t] = jnp.where(odd == 1, 2 * t, 2 * ((t % COLUMNS) * lines + t // COLUMNS))
    for part in small:
        part.wait()
    fill_weights(
        columns,
        second_buf,
        first_both,
        first_low,
        second,
        left_ref[...],
        right_ref[...],
        uptake_ref[...],
        gain_ref[...],
        loss_ref[...],
    )
    top_row = lax.broadcasted_iota(I32, (rows, bins), 0) % cells == 0
    wind = wind_ref[...]
    vapour = vapour_ref[...]
    wind_top_ref[...] = rows_of_lanes(wind_ref[0:1, :], bins)
    upwind = upwind_ref[pl.ds(start // 128, 1), :]
    block_bits = blocks.bit_length() - 1
    relative = ((upwind >> block_bits) - owner + 1 + wide_count) & (wide_count - 1)
    far = (relative << block_bits) + (upwind & (blocks - 1))
    near = blocks + (lax.broadcasted_iota(I32, far.shape, 1) & (blocks - 1))
    source_ref[...] = jnp.where(first, far, near)
    for copy in [window_copy] + copies:
        copy.wait()
    for g in range(blocks // group):
        x = haze_buf[g * group : (g + 1) * group].reshape(rows, bins)
        ids = range(g * group, (g + 1) * group)
        vapour_rows = jnp.concatenate([column_rows(vapour, b, cells, bins) for b in ids], 0)
        wind_rows = jnp.concatenate([column_rows(wind, b, cells, bins) for b in ids], 0)
        grown = grow(x, vapour_rows, first_both, first_low, second, rank)
        upwind = jnp.where(top_row, 0.0, pltpu.roll(grown, 1, 0))
        moved = grown - wind_rows * (grown - upwind)
        for j, b in enumerate(ids):
            at = j * cells
            target = window[0, start - base + b]
            slot = used[target]
            used[target] = slot + 1
            slot_ref[b] = slot
            packed_ref[slot] = moved[at : at + cells, :]
            top_ref[b : b + 1, :] = moved[at : at + 1, :]


def inflow_kernel(
    packed_in,
    top_ref,
    wind_top_ref,
    same_ref,
    low_ref,
    high_ref,
    slot_ref,
    source_ref,
    packed_hbm,
    near,
    inflow,
    sem,
):
    blocks, bins = top_ref.shape
    near[0:blocks, :] = low_ref[...]
    near[blocks : 2 * blocks, :] = same_ref[...]
    near[2 * blocks :, :] = high_ref[...]
    offset = (lax.axis_index("wide") * blocks) % 128
    for b in range(blocks):
        inflow[b : b + 1, :] = near[pl.ds(source_ref[0, offset + b], 1), :]
    inflow[...] = top_ref[...] + wind_top_ref[...] * inflow[...]
    for b in range(blocks):
        pltpu.make_async_copy(inflow.at[b], packed_hbm.at[slot_ref[b], 0], sem).start()
    pltpu.make_async_copy(inflow, packed_hbm.at[pl.ds(0, blocks), 0, :], sem).wait()


def place_kernel(arrived_ref, out_hbm, sem):
    wide_count = lax.axis_size("wide")
    lines = wide_count // COLUMNS
    odd = lax.axis_index("narrow") & 1
    for p in range(wide_count):
        source = jnp.where(odd == 1, p, (p % lines) * COLUMNS + p // lines)
        pltpu.make_async_copy(
            arrived_ref.at[pl.ds(2 * p, 2)], out_hbm.at[pl.ds(2 * source, 2)], sem
        ).start()
    pltpu.make_async_copy(arrived_ref, out_hbm, sem).wait()


def vapour_kernel(haze_ref, vapour_ref, uptake_ref, vapour_out_ref):
    blocks, cells, bins = haze_ref.shape
    vapour = vapour_ref[...]
    weights = jnp.broadcast_to(uptake_ref[...] * (1.0 / bins), (bins, bins)).T
    lane = lax.broadcasted_iota(I32, (cells, blocks), 1)
    out = jnp.zeros((cells, blocks), F32)
    for g in range(0, blocks, 8):
        mean_take = precise_dot(haze_ref[g : g + 8].reshape(8 * cells, bins), weights)
        for j in range(8):
            part = mean_take[j * cells : (j + 1) * cells, :blocks]
            out = jnp.where(lane == g + j, part, out)
    vapour_out_ref[...] = vapour * (1.0 / (1.0 + vapour * out))


def whole(space=VMEM):
    return pl.BlockSpec(memory_space=space)


def cost(flops, moved):
    return pl.CostEstimate(flops=flops, bytes_accessed=moved, transcendentals=0)


def local(
    haze_bin_mass,
    wind_speed,
    vapour,
    uptake_rates,
    coag_left,
    coag_right,
    coag_gain,
    coag_loss,
    targets,
    upwind_blocks,
):
    wide_count = lax.axis_size("wide")
    narrow_count = lax.axis_size("narrow")
    blocks, cells, bins = haze_bin_mass.shape
    slots = 2 * wide_count
    vapour_t = vapour.T
    uptake_row = uptake_rates[None, :]
    rates = (uptake_row, coag_left.T, coag_right.T, coag_gain, coag_loss)
    def shape(*dims, kind=F32):
        return jax.ShapeDtypeStruct(dims, kind)

    weight_scratch = [
        pltpu.VMEM((2 * bins, bins), F32),
        pltpu.VMEM((SEGMENT, 2 * bins), F32),
        pltpu.VMEM((2 * bins, 2 * bins), BF16),
        pltpu.VMEM((bins, 2 * bins), BF16),
        pltpu.VMEM((bins, 2 * bins), BF16),
    ]
    rows_type = shape(blocks, bins)
    rim = pl.pallas_call(
        rim_kernel,
        out_shape=rows_type,
        in_specs=[whole(pl.ANY)] * 7,
        out_specs=whole(),
        scratch_shapes=[
            pltpu.VMEM((blocks, bins), F32),
            pltpu.VMEM(vapour_t.shape, F32),
            *[pltpu.VMEM(rate.shape, F32) for rate in rates],
            *weight_scratch,
            pltpu.SemaphoreType.DMA,
            pltpu.SemaphoreType.DMA((6,)),
        ],
        cost_estimate=cost(10000000, 100000),
    )(haze_bin_mass, vapour_t, *rates)
    both = ("wide", "narrow")
    last = narrow_count - 1

    def flat(w, n):
        return (w % wide_count) * narrow_count + n % narrow_count

    def passed(distance):
        if distance == 0:
            route = [
                (flat(w, n), flat(w, n + 1)) for w in range(wide_count) for n in range(narrow_count)
            ]
        else:
            route = [(flat(w, last), flat(w + distance, 0)) for w in range(wide_count)]
        return lax.ppermute(rim, both, route)

    same, low, high = passed(0), passed(1), passed(-1)
    packed_type = shape(slots, cells, bins)
    upwind_rows = upwind_blocks.reshape(-1, 128)
    packed, top, wind_top, slot, source = pl.pallas_call(
        pack_kernel,
        out_shape=(packed_type, rows_type, rows_type, shape(blocks, kind=I32), shape(1, 128, kind=I32)),
        in_specs=[whole(pl.ANY)] * 10,
        out_specs=(whole(),) * 3 + (whole(pltpu.SMEM), whole()),
        scratch_shapes=[
            pltpu.VMEM((blocks, cells, bins), F32),
            pltpu.VMEM(vapour_t.shape, F32),
            pltpu.VMEM(vapour_t.shape, F32),
            *[pltpu.VMEM(rate.shape, F32) for rate in rates],
            pltpu.VMEM(upwind_rows.shape, I32),
            *weight_scratch,
            pltpu.SMEM((1, 128), I32),
            pltpu.SMEM((wide_count,), I32),
            pltpu.SemaphoreType.DMA((blocks // 64,)),
            pltpu.SemaphoreType.DMA,
            pltpu.SemaphoreType.DMA((8,)),
        ],
        cost_estimate=cost(800000000, 4000000),
        compiler_params=pltpu.CompilerParams(vmem_limit_bytes=67043328),
    )(haze_bin_mass, wind_speed.T, vapour_t, *rates, upwind_rows, targets.T)
    packed = pl.pallas_call(
        inflow_kernel,
        out_shape=packed_type,
        in_specs=[whole(pl.ANY)] + [whole()] * 5 + [whole(pltpu.SMEM)] * 2,
        out_specs=whole(pl.ANY),
        scratch_shapes=[
            pltpu.VMEM((3 * blocks, bins), F32),
            pltpu.VMEM((blocks, bins), F32),
            pltpu.SemaphoreType.DMA,
        ],
        input_output_aliases={0: 0},
        cost_estimate=cost(100000, 300000),
    )(packed, top, wind_top, same, low, high, slot, source)
    lines = wide_count // COLUMNS
    order = [line * COLUMNS + column for column in range(COLUMNS) for line in range(lines)]
    groups = [
        [w * narrow_count + n for w in (range(wide_count) if n % 2 else order)]
        for n in range(narrow_count)
    ]
    arrived = lax.all_to_all(
        packed, both, split_axis=0, concat_axis=0, tiled=True, axis_index_groups=groups
    )
    haze_output_slots = pl.pallas_call(
        place_kernel,
        out_shape=packed_type,
        in_specs=[whole(pl.ANY)],
        out_specs=whole(pl.ANY),
        scratch_shapes=[pltpu.SemaphoreType.DMA],
        cost_estimate=cost(0, 4000000),
        compiler_params=pltpu.CompilerParams(vmem_limit_bytes=1048576),
    )(arrived)
    vapour_out = pl.pallas_call(
        vapour_kernel,
        out_shape=shape(cells, blocks),
        in_specs=[whole()] * 3,
        out_specs=whole(),
        cost_estimate=cost(400000000, 1000000),
    )(haze_bin_mass, vapour_t, uptake_row)
    return (haze_output_slots, vapour_out.T)


def solution(mesh):
    in_specs = (
        P("wide", "narrow", None),
        P("wide", "narrow"),
        P("wide", "narrow"),
        P(),
        P(),
        P(),
        P(),
        P(),
        P(),
        P(),
    )
    out_specs = (P("wide", "narrow", None), P("wide", "narrow"))
    return jax.shard_map(local, mesh=mesh, in_specs=in_specs, out_specs=out_specs, check_vma=False)
```

```python
import jax
import jax.numpy as jnp
from jax import lax
from jax.experimental import pallas as pl
from jax.experimental.pallas import tpu as pltpu
from jax.sharding import PartitionSpec as P

HIGHEST = lax.Precision.HIGHEST
STEP_DT = 0.25
F32 = jnp.float32
BF16 = jnp.bfloat16
I32 = jnp.int32
VMEM = pltpu.VMEM
SEGMENT = 32
TAKE_LANE = 24
COLUMNS = 8


def precise_dot(a, b):
    return jnp.dot(a, b, precision=HIGHEST, preferred_element_type=F32)


def split(x):
    high = x.astype(BF16)
    return high, (x - high.astype(F32)).astype(BF16)


def column_rows(table, column, rows, lanes):
    return jnp.broadcast_to(table[:, column : column + 1], (rows, lanes))


def rows_of_lanes(row, lanes):
    count = row.shape[1]
    shape = (count, count)
    eye = lax.broadcasted_iota(I32, shape, 0) == lax.broadcasted_iota(I32, shape, 1)
    spread = jnp.where(eye, jnp.broadcast_to(row, shape), 0.0)
    return precise_dot(spread, jnp.ones((count, lanes), F32))


def fill_weights(columns, second, first_both, first_low, second_ref, left, right, uptake, gain, loss):
    rank, bins = left.shape
    columns[...] = jnp.zeros_like(columns)
    for at in range(0, 3 * SEGMENT, SEGMENT):
        columns[at : at + rank, :] = left
        columns[at + rank : at + 2 * rank, :] = left
        columns[at + TAKE_LANE : at + TAKE_LANE + 1, :] = uptake * (1.0 / bins)
        columns[bins + at : bins + at + rank, :] = right
    for k in range(0, 2 * bins, bins):
        high, low = split(columns[k : k + bins, :].T)
        first_both[0:bins, k : k + bins] = high
        first_both[bins:, k : k + bins] = high
        first_low[:, k : k + bins] = low
    second[...] = jnp.zeros_like(second)
    second[0:rank, 0:bins] = STEP_DT * gain
    second[rank : 2 * rank, bins:] = STEP_DT * loss
    second[TAKE_LANE : TAKE_LANE + 1, bins:] = -uptake
    high, low = split(second[...])
    second_ref[0:SEGMENT, :] = high
    second_ref[SEGMENT : 2 * SEGMENT, :] = low
    second_ref[2 * SEGMENT : 3 * SEGMENT, :] = high
    second_ref[3 * SEGMENT :, :] = jnp.zeros_like(high)


def grow(x, vapour_rows, first_both, first_low, second, rank):
    rows, bins = x.shape
    lane = lax.broadcasted_iota(I32, (rows, bins), 1)
    place = lane & (SEGMENT - 1)
    one_lanes = jnp.where((place >= rank) & (place < 2 * rank), 1.0, 0.0).astype(F32)
    high, low = split(x)
    proj = jnp.dot(jnp.concatenate([high, low], 1), first_both[...], preferred_element_type=F32)
    proj = proj + jnp.dot(high, first_low[...], preferred_element_type=F32)
    left, right = proj[:, :bins], proj[:, bins:]
    taken = vapour_rows / (1.0 + vapour_rows * left)
    product = jnp.where(place == TAKE_LANE, taken, left * (right + one_lanes))
    product = jnp.where(lane < 3 * SEGMENT, product, 0.0)
    high, low = split(product)
    parts = jnp.where(lane < 2 * SEGMENT, high.astype(F32), low.astype(F32)).astype(BF16)
    rate = jnp.dot(parts, second[...], preferred_element_type=F32)
    return x + (rate[:, :bins] - x * rate[:, bins:])


def fetched(sources, targets, sems):
    copies = []
    for i, (source, target) in enumerate(zip(sources, targets, strict=True)):
        copy = pltpu.make_async_copy(source, target, sems.at[i])
        copy.start()
        copies.append(copy)
    return copies


def rim_kernel(
    haze_hbm,
    vapour_hbm,
    uptake_hbm,
    left_hbm,
    right_hbm,
    gain_hbm,
    loss_hbm,
    rim_ref,
    rows_buf,
    vapour_ref,
    uptake_ref,
    left_ref,
    right_ref,
    gain_ref,
    loss_ref,
    columns,
    second_buf,
    first_both,
    first_low,
    second,
    sem,
    small_sems,
):
    cells = haze_hbm.shape[1]
    copy = pltpu.make_async_copy(haze_hbm.at[:, cells - 1, :], rows_buf, sem)
    copy.start()
    small = fetched(
        (vapour_hbm, uptake_hbm, left_hbm, right_hbm, gain_hbm, loss_hbm),
        (vapour_ref, uptake_ref, left_ref, right_ref, gain_ref, loss_ref),
        small_sems,
    )
    for part in small:
        part.wait()
    fill_weights(
        columns,
        second_buf,
        first_both,
        first_low,
        second,
        left_ref[...],
        right_ref[...],
        uptake_ref[...],
        gain_ref[...],
        loss_ref[...],
    )
    vapour_rows = rows_of_lanes(vapour_ref[cells - 1 : cells, :], rows_buf.shape[1])
    copy.wait()
    rim_ref[...] = grow(
        rows_buf[...], vapour_rows, first_both, first_low, second, left_ref.shape[0]
    )


def pack_kernel(
    haze_hbm,
    wind_hbm,
    vapour_hbm,
    uptake_hbm,
    left_hbm,
    right_hbm,
    gain_hbm,
    loss_hbm,
    upwind_hbm,
    targets_hbm,
    packed_ref,
    top_ref,
    wind_top_ref,
    slot_ref,
    source_ref,
    haze_buf,
    wind_ref,
    vapour_ref,
    uptake_ref,
    left_ref,
    right_ref,
    gain_ref,
    loss_ref,
    upwind_ref,
    columns,
    second_buf,
    first_both,
    first_low,
    second,
    window,
    used,
    haze_sems,
    window_sem,
    small_sems,
):
    blocks, cells, bins = haze_buf.shape
    rank = left_ref.shape[0]
    group = 64
    rows = group * cells
    wide_count = lax.axis_size("wide")
    owner = lax.axis_index("wide")
    first = lax.axis_index("narrow") == 0
    start = owner * blocks
    base = pl.multiple_of((start // 128) * 128, 128)
    window_copy = pltpu.make_async_copy(
        targets_hbm.at[:, pl.ds(base, 128)], window, window_sem
    )
    window_copy.start()
    copies = []
    for g in range(blocks // group):
        part = pl.ds(g * group, group)
        copy = pltpu.make_async_copy(haze_hbm.at[part], haze_buf.at[part], haze_sems.at[g])
        copy.start()
        copies.append(copy)
    small = fetched(
        (wind_hbm, vapour_hbm, uptake_hbm, left_hbm, right_hbm, gain_hbm, loss_hbm, upwind_hbm),
        (wind_ref, vapour_ref, uptake_ref, left_ref, right_ref, gain_ref, loss_ref, upwind_ref),
        small_sems,
    )
    packed_ref[...] = jnp.zeros_like(packed_ref)
    lines = wide_count // COLUMNS
    odd = lax.axis_index("narrow") & 1
    for t in range(wide_count):
        used[t] = jnp.where(odd == 1, 2 * t, 2 * ((t % COLUMNS) * lines + t // COLUMNS))
    for part in small:
        part.wait()
    fill_weights(
        columns,
        second_buf,
        first_both,
        first_low,
        second,
        left_ref[...],
        right_ref[...],
        uptake_ref[...],
        gain_ref[...],
        loss_ref[...],
    )
    top_row = lax.broadcasted_iota(I32, (rows, bins), 0) % cells == 0
    wind = wind_ref[...]
    vapour = vapour_ref[...]
    wind_top_ref[...] = rows_of_lanes(wind_ref[0:1, :], bins)
    upwind = upwind_ref[pl.ds(start // 128, 1), :]
    block_bits = blocks.bit_length() - 1
    relative = ((upwind >> block_bits) - owner + 1 + wide_count) & (wide_count - 1)
    far = (relative << block_bits) + (upwind & (blocks - 1))
    near = blocks + (lax.broadcasted_iota(I32, far.shape, 1) & (blocks - 1))
    source_ref[...] = jnp.where(first, far, near)
    for copy in [window_copy] + copies:
        copy.wait()
    for g in range(blocks // group):
        x = haze_buf[g * group : (g + 1) * group].reshape(rows, bins)
        ids = range(g * group, (g + 1) * group)
        vapour_rows = jnp.concatenate([column_rows(vapour, b, cells, bins) for b in ids], 0)
        wind_rows = jnp.concatenate([column_rows(wind, b, cells, bins) for b in ids], 0)
        grown = grow(x, vapour_rows, first_both, first_low, second, rank)
        upwind = jnp.where(top_row, 0.0, pltpu.roll(grown, 1, 0))
        moved = grown - wind_rows * (grown - upwind)
        for j, b in enumerate(ids):
            at = j * cells
            target = window[0, start - base + b]
            slot = used[target]
            used[target] = slot + 1
            slot_ref[b] = slot
            packed_ref[slot] = moved[at : at + cells, :]
            top_ref[b : b + 1, :] = moved[at : at + 1, :]


def inflow_kernel(
    packed_in,
    top_ref,
    wind_top_ref,
    same_ref,
    high_ref,
    low_ref,
    slot_ref,
    source_ref,
    packed_hbm,
    near,
    inflow,
    sem,
):
    blocks, bins = top_ref.shape
    near[0:blocks, :] = low_ref[...]
    near[blocks : 2 * blocks, :] = same_ref[...]
    near[2 * blocks :, :] = high_ref[...]
    offset = (lax.axis_index("wide") * blocks) % 128
    for b in range(blocks):
        inflow[b : b + 1, :] = near[pl.ds(source_ref[0, offset + b], 1), :]
    inflow[...] = top_ref[...] + wind_top_ref[...] * inflow[...]
    for b in range(blocks):
        pltpu.make_async_copy(inflow.at[b], packed_hbm.at[slot_ref[b], 0], sem).start()
    pltpu.make_async_copy(inflow, packed_hbm.at[pl.ds(0, blocks), 0, :], sem).wait()


def place_kernel(arrived_ref, out_hbm, sem):
    wide_count = lax.axis_size("wide")
    lines = wide_count // COLUMNS
    odd = lax.axis_index("narrow") & 1
    for p in range(wide_count):
        source = jnp.where(odd == 1, p, (p % lines) * COLUMNS + p // lines)
        pltpu.make_async_copy(
            arrived_ref.at[pl.ds(2 * p, 2)], out_hbm.at[pl.ds(2 * source, 2)], sem
        ).start()
    pltpu.make_async_copy(arrived_ref, out_hbm, sem).wait()


def vapour_kernel(haze_ref, vapour_ref, uptake_ref, vapour_out_ref):
    blocks, cells, bins = haze_ref.shape
    vapour = vapour_ref[...]
    weights = jnp.broadcast_to(uptake_ref[...] * (1.0 / bins), (bins, bins)).T
    lane = lax.broadcasted_iota(I32, (cells, blocks), 1)
    out = jnp.zeros((cells, blocks), F32)
    for g in range(0, blocks, 8):
        mean_take = precise_dot(haze_ref[g : g + 8].reshape(8 * cells, bins), weights)
        for j in range(8):
            part = mean_take[j * cells : (j + 1) * cells, :blocks]
            out = jnp.where(lane == g + j, part, out)
    vapour_out_ref[...] = vapour * (1.0 / (1.0 + vapour * out))


def whole(space=VMEM):
    return pl.BlockSpec(memory_space=space)


def cost(flops, moved):
    return pl.CostEstimate(flops=flops, bytes_accessed=moved, transcendentals=0)


def local(
    haze_bin_mass,
    wind_speed,
    vapour,
    uptake_rates,
    coag_left,
    coag_right,
    coag_gain,
    coag_loss,
    targets,
    upwind_blocks,
):
    wide_count = lax.axis_size("wide")
    narrow_count = lax.axis_size("narrow")
    blocks, cells, bins = haze_bin_mass.shape
    slots = 2 * wide_count
    vapour_t = vapour.T
    uptake_row = uptake_rates[None, :]
    rates = (uptake_row, coag_left.T, coag_right.T, coag_gain, coag_loss)
    def shape(*dims, kind=F32):
        return jax.ShapeDtypeStruct(dims, kind)

    weight_scratch = [
        pltpu.VMEM((2 * bins, bins), F32),
        pltpu.VMEM((SEGMENT, 2 * bins), F32),
        pltpu.VMEM((2 * bins, 2 * bins), BF16),
        pltpu.VMEM((bins, 2 * bins), BF16),
        pltpu.VMEM((bins, 2 * bins), BF16),
    ]
    rows_type = shape(blocks, bins)
    rim = pl.pallas_call(
        rim_kernel,
        out_shape=rows_type,
        in_specs=[whole(pl.ANY)] * 7,
        out_specs=whole(),
        scratch_shapes=[
            pltpu.VMEM((blocks, bins), F32),
            pltpu.VMEM(vapour_t.shape, F32),
            *[pltpu.VMEM(rate.shape, F32) for rate in rates],
            *weight_scratch,
            pltpu.SemaphoreType.DMA,
            pltpu.SemaphoreType.DMA((6,)),
        ],
        cost_estimate=cost(10000000, 100000),
    )(haze_bin_mass, vapour_t, *rates)
    both = ("wide", "narrow")
    last = narrow_count - 1

    def flat(w, n):
        return (w % wide_count) * narrow_count + n % narrow_count

    def passed(distance):
        if distance == 0:
            route = [
                (flat(w, n), flat(w, n + 1)) for w in range(wide_count) for n in range(narrow_count)
            ]
        else:
            route = [(flat(w, last), flat(w + distance, 0)) for w in range(wide_count)]
        return lax.ppermute(rim, both, route)

    same, high, low = passed(0), passed(-1), passed(1)
    packed_type = shape(slots, cells, bins)
    upwind_rows = upwind_blocks.reshape(-1, 128)
    packed, top, wind_top, slot, source = pl.pallas_call(
        pack_kernel,
        out_shape=(packed_type, rows_type, rows_type, shape(blocks, kind=I32), shape(1, 128, kind=I32)),
        in_specs=[whole(pl.ANY)] * 10,
        out_specs=(whole(),) * 3 + (whole(pltpu.SMEM), whole()),
        scratch_shapes=[
            pltpu.VMEM((blocks, cells, bins), F32),
            pltpu.VMEM(vapour_t.shape, F32),
            pltpu.VMEM(vapour_t.shape, F32),
            *[pltpu.VMEM(rate.shape, F32) for rate in rates],
            pltpu.VMEM(upwind_rows.shape, I32),
            *weight_scratch,
            pltpu.SMEM((1, 128), I32),
            pltpu.SMEM((wide_count,), I32),
            pltpu.SemaphoreType.DMA((blocks // 64,)),
            pltpu.SemaphoreType.DMA,
            pltpu.SemaphoreType.DMA((8,)),
        ],
        cost_estimate=cost(800000000, 4000000),
        compiler_params=pltpu.CompilerParams(vmem_limit_bytes=67043328),
    )(haze_bin_mass, wind_speed.T, vapour_t, *rates, upwind_rows, targets.T)
    packed = pl.pallas_call(
        inflow_kernel,
        out_shape=packed_type,
        in_specs=[whole(pl.ANY)] + [whole()] * 5 + [whole(pltpu.SMEM)] * 2,
        out_specs=whole(pl.ANY),
        scratch_shapes=[
            pltpu.VMEM((3 * blocks, bins), F32),
            pltpu.VMEM((blocks, bins), F32),
            pltpu.SemaphoreType.DMA,
        ],
        input_output_aliases={0: 0},
        cost_estimate=cost(100000, 300000),
    )(packed, top, wind_top, same, high, low, slot, source)
    lines = wide_count // COLUMNS
    order = [line * COLUMNS + column for column in range(COLUMNS) for line in range(lines)]
    groups = [
        [w * narrow_count + n for w in (range(wide_count) if n % 2 else order)]
        for n in range(narrow_count)
    ]
    arrived = lax.all_to_all(
        packed, both, split_axis=0, concat_axis=0, tiled=True, axis_index_groups=groups
    )
    haze_output_slots = pl.pallas_call(
        place_kernel,
        out_shape=packed_type,
        in_specs=[whole(pl.ANY)],
        out_specs=whole(pl.ANY),
        scratch_shapes=[pltpu.SemaphoreType.DMA],
        cost_estimate=cost(0, 4000000),
        compiler_params=pltpu.CompilerParams(vmem_limit_bytes=1048576),
    )(arrived)
    vapour_out = pl.pallas_call(
        vapour_kernel,
        out_shape=shape(cells, blocks),
        in_specs=[whole()] * 3,
        out_specs=whole(),
        cost_estimate=cost(400000000, 1000000),
    )(haze_bin_mass, vapour_t, uptake_row)
    return (haze_output_slots, vapour_out.T)


def solution(mesh):
    in_specs = (
        P("wide", "narrow", None),
        P("wide", "narrow"),
        P("wide", "narrow"),
        P(),
        P(),
        P(),
        P(),
        P(),
        P(),
        P(),
    )
    out_specs = (P("wide", "narrow", None), P("wide", "narrow"))
    return jax.shard_map(local, mesh=mesh, in_specs=in_specs, out_specs=out_specs, check_vma=False)
```
